32 devices in a mesh: group: 2 (over x), row: 8 (over z, y), tp: 2 (over core).
Axes of the slice: x: 2, y: 2, z: 4, core: 2. Of those that a mesh axis runs over, the one named last changes fastest.
Arguments:
- prompt_latent: bfloat16 [16, 16, 128, 576], P(('group', 'row'), None, 'tp'), parts along dimension 0, may hold values from -6 to 6
- row_cache: bfloat16 [32, 256, 576], P(('group', 'row')), parts along dimension 0, may hold values from -24 to 24
- queries: bfloat16 [4, 32, 128, 576], P(None, ('group', 'row'), 'tp'), parts along dimension 1, may hold values from -80 to 80
- new_latent: bfloat16 [4, 32, 576], P(None, ('group', 'row')), parts along dimension 1, may hold values from -12 to 12
- prompt_len: int32 [32], P('group'), parts along dimension 0, may hold values from 1 to 1024, 12288 in all
- assign: int32 [32], P('group'), parts along dimension 0, may hold values from 0 to 15, as said below
- row_ctx: int32 [32], P(('group', 'row')), parts along dimension 0, may hold values from 2 to 256
Outputs:
- attended: bfloat16 [4, 32, 128, 512], P(None, ('group', 'row'), 'tp'), parts along dimension 1
The draws below stay inside these ranges and needn't reach their ends.
There are 2 independent parts, one for each index of `group`. The reference program is written for one: setup_inputs(seed, part) draws one part's arguments, and reference() takes and returns one part's arrays. A program takes and returns all parts, laid end to end along the dimension named above; each array names one. Nothing has to cross between parts.
Inputs may be any that keep to these rules, and one draw needn't show every extreme that they name: `prompt_len`: latents at positions from a prompt's length on are not part of that prompt. Decode row r continues prompt assign[r]; every prompt goes to exactly one row. Prompt p belongs to prompt group p // 16; the rows of one index of row take at most 2 prompts of any one prompt group. Row r's cached latents are its first row_ctx[r] positions.
All inputs are finite; a program needn't handle non-finite values.
Results may differ from the reference program's by a relative error of at most 0.0044.
Values may be sent and summed in bfloat16 or wider, within the bound.
A program may use at most 128 MiB of HBM per device.

```python
import math
import jax
import jax.numpy as jnp
import numpy as np
from jax import lax

HEADS = 128
KV_RANK = 512
ROPE_DIM = 64
NOPE_DIM = 128
ROWS_DEV = 2
LMAX = 1024
CMAX = 256
STEPS = 4
SPR = 8
ROWS = 16
MOST = 2
N_ROW = 8


def joint_rows(key):
    base_key = jax.random.fold_in(key, 4242)
    key_cache, key_query = jax.random.split(base_key, 2)
    latent_width = KV_RANK + ROPE_DIM
    cache_rows = jnp.clip(jax.random.normal(key_cache, (ROWS, CMAX, latent_width), jnp.float32), -6.0, 6.0)
    query_rows = 1.5 * jnp.clip(jax.random.normal(key_query, (STEPS, ROWS, HEADS, latent_width), jnp.float32), -6.0, 6.0)
    return (cache_rows, query_rows)


def draw_row_cache(key, part):
    return joint_rows(key)[0].astype(jnp.bfloat16)


def draw_queries(key, part):
    return joint_rows(key)[1].astype(jnp.bfloat16)


def draw_assign(key, part):
    base_key = jax.random.fold_in(key, 7717)
    key_anchor, key_blocks, key_slots, key_order = jax.random.split(base_key, 4)
    group_total = N_ROW // SPR
    block_total = ROWS_DEV // MOST
    stride_groups = group_total // block_total
    anchor = jax.random.randint(key_anchor, (), 0, N_ROW).astype(jnp.int32)
    block_keys = jax.random.split(key_blocks, block_total)
    slot_keys = jax.random.split(key_slots, ROWS_DEV)
    devices = jnp.arange(N_ROW, dtype=jnp.int32)
    relative = (devices - anchor) % N_ROW
    columns = []
    for slot_id in range(ROWS_DEV):
        block_id = slot_id // MOST
        block_perm = jax.random.permutation(block_keys[block_id], N_ROW).astype(jnp.int32)
        others = 1 + jax.random.permutation(slot_keys[slot_id], N_ROW - 1).astype(jnp.int32)
        fixed_first = jnp.concatenate([jnp.zeros((1,), jnp.int32), others], 0)
        moved_device = (jnp.take(fixed_first, relative) + anchor) % N_ROW
        chosen = jnp.take(block_perm, moved_device)
        columns.append(chosen % stride_groups * block_total + block_id)
    group_label = jnp.stack(columns, 1).reshape(ROWS).astype(jnp.int32)
    order_key = group_label * ROWS + jax.random.permutation(key_order, ROWS).astype(jnp.int32)
    order = jnp.argsort(order_key)
    return jnp.zeros((ROWS,), jnp.int32).at[order].set(jnp.arange(ROWS, dtype=jnp.int32))


def with_ends(array, key, smallest, largest):
    longest = array.shape.index(max(array.shape))
    spots = []
    for shift in (0, 1):
        where = [jax.random.randint(jax.random.fold_in(key, axis), (), 0, length) for axis, length in enumerate(array.shape)]
        where[longest] = (where[longest] + shift) % array.shape[longest]
        spots.append(tuple(where))
    return array.at[spots[0]].set(smallest).at[spots[1]].set(largest)


def block_levels(rng, shape, cuts, least, top_value):
    gain = 1.0
    for dim, parts in cuts:
        steps = jax.random.uniform(jax.random.fold_in(jax.random.fold_in(rng, 6), dim), (parts,), jnp.float32, least / len(cuts), top_value / len(cuts))
        gain = gain * jnp.repeat(jnp.exp(steps), shape[dim] // parts).reshape((-1,) + (1,) * (len(shape) - 1 - dim))
    return gain


def split_up(count, total, reach, skew):
    loads = [(1 << 20) // math.isqrt(standing ** skew) + 1 for standing in range(2, count + 1)]
    spare, holding = total - reach - (count - 1), [1] * (count - 1)
    while spare > 0:
        free = [i for i in range(count - 1) if holding[i] < reach]
        mass, budget = sum([loads[i] for i in free]), spare
        for i in free:
            extra = min(reach - holding[i], max(1, budget * loads[i] // mass), spare)
            holding[i] = holding[i] + extra
            spare = spare - extra
    return np.array([reach] + holding)


def uneven(stream_key, count, total, bound, slope):
    if count == 2:
        one = jax.random.randint(stream_key, (), max(1, total - bound), min(bound, total - 1) + 1)
        return jnp.stack([one, total - one])
    sizes = jnp.asarray(split_up(count, total, bound, slope), jnp.int32)
    couples = (count - 1) // 2
    source_of, sink = sizes[1:1 + 2 * couples:2], sizes[2:2 + 2 * couples:2]
    margin = jnp.minimum(source_of - 1, bound - sink)
    moved = jax.random.randint(jax.random.fold_in(stream_key, 1), (couples,), 0, 1 << 20) % (margin + 1)
    sizes = sizes.at[1:1 + 2 * couples:2].set(source_of - moved).at[2:2 + 2 * couples:2].set(sink + moved)
    return sizes[jax.random.permutation(jax.random.fold_in(stream_key, 2), count)]


def noise(key, extent, scale, reach, cuts=(), held_as=jnp.bfloat16):
    drawn = jax.random.normal(key, extent, jnp.float32) * scale
    if len(cuts) > 0:
        drawn = block_levels(key, extent, cuts, -0.22, 0.18) * drawn
    return jnp.clip(drawn, min=-reach, max=reach).astype(held_as)


def setup_inputs(seed: int = 0, part: int = 0) -> dict:
    key_list = jax.random.split(jax.random.key(seed), 8)
    own_keys = jax.random.split(jax.random.fold_in(key_list[7], part), 8)
    prompt_latent = noise(own_keys[0], (N_ROW, ROWS_DEV * SPR, LMAX // SPR, KV_RANK + ROPE_DIM), 1.0, 6.0, ((0, 8), (2, 2)))
    row_cache = draw_row_cache(jax.random.fold_in(jax.random.fold_in(key_list[7], part), 71), part)
    queries = draw_queries(jax.random.fold_in(jax.random.fold_in(key_list[7], part), 71), part)
    new_latent = noise(own_keys[3], (STEPS, ROWS, KV_RANK + ROPE_DIM), 2.0, 12.0, ((1, 8),))
    prompt_len = uneven(own_keys[4], ROWS, ROWS * LMAX * 3 // 4, LMAX, 2).astype(jnp.int32)
    assign = draw_assign(jax.random.fold_in(jax.random.fold_in(key_list[7], part), 71), part)
    row_ctx = with_ends(jax.random.randint(own_keys[6], (ROWS,), 2, CMAX + 1), jax.random.fold_in(own_keys[6], 1), 2, CMAX).astype(jnp.int32)
    return {"prompt_latent": prompt_latent, "row_cache": row_cache, "queries": queries, "new_latent": new_latent, "prompt_len": prompt_len, "assign": assign, "row_ctx": row_ctx}


def reference(prompt_latent, row_cache, queries, new_latent, prompt_len, assign, row_ctx):
    scale_factor = (NOPE_DIM + ROPE_DIM) ** -0.5
    steps_idx = jnp.arange(STEPS, dtype=jnp.int32)
    causal = steps_idx[None, :] <= steps_idx[:, None]
    group_rows = ROWS_DEV * SPR
    latent_width = KV_RANK + ROPE_DIM
    zero_index = jnp.zeros((), jnp.int32)

    def one_row(row_index):
        prompt_id = assign[row_index].astype(jnp.int32)
        group_id = (prompt_id // group_rows).astype(jnp.int32)
        inner_id = (prompt_id - group_id * group_rows).astype(jnp.int32)
        prompt_keys = lax.dynamic_slice(prompt_latent, (group_id * SPR, inner_id, zero_index, zero_index),
                                        (SPR, 1, LMAX // SPR, latent_width)).reshape(LMAX, latent_width)
        live_len = lax.dynamic_index_in_dim(prompt_len, prompt_id, 0, keepdims=False)
        cache_keys = lax.dynamic_index_in_dim(row_cache, row_index, 0, keepdims=False)
        cache_len = lax.dynamic_index_in_dim(row_ctx, row_index, 0, keepdims=False)
        query_rows = lax.dynamic_index_in_dim(queries, row_index, 1, keepdims=False)
        fresh_keys = lax.dynamic_index_in_dim(new_latent, row_index, 1, keepdims=False)
        all_keys = jnp.concatenate([prompt_keys, cache_keys, fresh_keys], 0).astype(jnp.float32)
        scores = jnp.einsum("shc,kc->shk", query_rows.astype(jnp.float32), all_keys) * scale_factor
        prompt_mask = jnp.arange(LMAX, dtype=jnp.int32) < live_len
        cache_mask = jnp.arange(CMAX, dtype=jnp.int32) < cache_len
        full_mask = jnp.concatenate([jnp.broadcast_to(prompt_mask[None, :], (STEPS, LMAX)),
                                     jnp.broadcast_to(cache_mask[None, :], (STEPS, CMAX)), causal], 1)
        scores = jnp.where(full_mask[:, None, :], scores, -jnp.inf)
        row_top = jnp.max(scores, axis=2, keepdims=True)
        exponent = jnp.exp(scores - row_top)
        weights = (exponent / jnp.sum(exponent, axis=2, keepdims=True)).astype(jnp.bfloat16)
        values = all_keys[:, :KV_RANK]
        return jnp.einsum("shk,kc->shc", weights.astype(jnp.float32), values).astype(jnp.bfloat16)

    result = lax.map(one_row, jnp.arange(ROWS, dtype=jnp.int32))
    return jnp.transpose(result, (1, 0, 2, 3))
```

```python
import functools

import jax
import jax.numpy as jnp
from jax import lax
from jax.experimental import pallas as pl
from jax.experimental.pallas import tpu as pltpu
from jax.sharding import PartitionSpec as P

KV_RANK = 512
ROPE_DIM = 64
NOPE_DIM = 128
SPR = 8


def pick(array, index):
    return lax.map(lambda i: lax.dynamic_index_in_dim(array, i, 0, keepdims=False), index)


def shards(prompt_latent, row_cache, queries, new_latent, prompt_len, assign, row_ctx):
    row_count = lax.axis_size("row")
    pair_count = lax.axis_size("tp")
    row_place = lax.axis_index("row")
    rows_here = row_cache.shape[0]
    group_rows = prompt_latent.shape[1]
    piece_len = prompt_latent.shape[2]
    latent_width = prompt_latent.shape[3]
    full_len = piece_len * SPR * pair_count
    most_slots = min(rows_here, max(2, 2 * rows_here * SPR // row_count))
    home_group = row_place // SPR
    dest_prompt = assign.reshape(row_count, rows_here)
    in_group = dest_prompt // group_rows == home_group
    row_ids = jnp.arange(rows_here, dtype=jnp.int32)
    up_to = row_ids[:, None] <= row_ids[None, :]
    rank = jnp.sum((in_group[:, :, None] & up_to[None]).astype(jnp.int32), axis=1) - 1
    slot_ids = jnp.arange(most_slots, dtype=jnp.int32)
    picked = in_group[:, :, None] & (rank[:, :, None] == slot_ids[None, None, :])
    local_id = dest_prompt - home_group * group_rows
    source_index = jnp.sum(jnp.where(picked, local_id[:, :, None], 0), axis=1)
    filled = jnp.any(picked, axis=1).reshape(-1)
    owned = lax.dynamic_slice_in_dim(assign, row_place * rows_here, rows_here)
    owned_group = owned // group_rows
    same_before = (owned_group[:, None] == owned_group[None, :]) & (
        row_ids[None, :] < row_ids[:, None]
    )
    own_rank = jnp.sum(same_before.astype(jnp.int32), axis=1)
    block_ids = jnp.arange(SPR, dtype=jnp.int32)
    fetch_index = (
        (owned_group[:, None] * SPR + block_ids[None, :]) * most_slots + own_rank[:, None]
    ).reshape(-1)
    local = prompt_latent[0]
    rows_taken = pick(local, source_index.reshape(-1))
    rows_taken = jnp.where(filled[:, None, None], rows_taken, jnp.zeros_like(rows_taken))
    moved = lax.all_to_all(
        rows_taken.reshape((row_count, most_slots) + local.shape[1:]),
        "row",
        split_axis=0,
        concat_axis=0,
        tiled=True,
    )
    flat = moved.reshape(row_count * most_slots, piece_len, latent_width)
    mine = pick(flat, fetch_index).reshape(rows_here, SPR, 1, piece_len, latent_width)
    paired = lax.all_gather(mine, "tp", axis=2, tiled=True)
    latents = paired.reshape(rows_here, full_len, latent_width)
    live_len = pick(prompt_len, owned)
    scale_factor = (NOPE_DIM + ROPE_DIM) ** (-0.5)
    steps_count = queries.shape[0]
    cache_len = row_cache.shape[1]
    cache_scores = (
        jnp.einsum("srhc,rkc->rshk", queries, row_cache, preferred_element_type=jnp.float32)
        * scale_factor
    )
    cache_live = jnp.arange(cache_len, dtype=jnp.int32)[None, :] < row_ctx[:, None]
    cache_scores = jnp.where(cache_live[:, None, None, :], cache_scores, -jnp.inf)
    fresh_scores = (
        jnp.einsum("srhc,jrc->rshj", queries, new_latent, preferred_element_type=jnp.float32)
        * scale_factor
    )
    step_ids = jnp.arange(steps_count, dtype=jnp.int32)
    causal = step_ids[None, :] <= step_ids[:, None]
    fresh_scores = jnp.where(causal[None, :, None, :], fresh_scores, -jnp.inf)
    prompt_live = jnp.arange(full_len, dtype=jnp.int32)[None, :] < live_len[:, None]
    prompt_scores = (
        jnp.einsum("srhc,rkc->rshk", queries, latents, preferred_element_type=jnp.float32)
        * scale_factor
    )
    prompt_scores = jnp.where(prompt_live[:, None, None, :], prompt_scores, -jnp.inf)
    row_top = jnp.maximum(
        jnp.max(prompt_scores, axis=3, keepdims=True),
        jnp.maximum(
            jnp.max(cache_scores, axis=3, keepdims=True),
            jnp.max(fresh_scores, axis=3, keepdims=True),
        ),
    )
    prompt_exp = jnp.exp(prompt_scores - row_top)
    cache_exp = jnp.exp(cache_scores - row_top)
    fresh_exp = jnp.exp(fresh_scores - row_top)
    denominator = (
        jnp.sum(prompt_exp, axis=3, keepdims=True)
        + jnp.sum(cache_exp, axis=3, keepdims=True)
        + jnp.sum(fresh_exp, axis=3, keepdims=True)
    )
    prompt_probs = (prompt_exp / denominator).astype(jnp.bfloat16)
    cache_probs = (cache_exp / denominator).astype(jnp.bfloat16)
    fresh_probs = (fresh_exp / denominator).astype(jnp.bfloat16)
    cache_out = jnp.einsum(
        "rshk,rkc->srhc", cache_probs, row_cache[:, :, :KV_RANK], preferred_element_type=jnp.float32
    )
    fresh_out = jnp.einsum(
        "rshj,jrc->srhc",
        fresh_probs,
        new_latent[:, :, :KV_RANK],
        preferred_element_type=jnp.float32,
    )
    prompt_out = jnp.einsum(
        "rshk,rkc->srhc", prompt_probs, latents[:, :, :KV_RANK], preferred_element_type=jnp.float32
    )
    return (prompt_out + cache_out + fresh_out).astype(jnp.bfloat16)


MESH = pl.DeviceIdType.MESH


SENDS = (
    ((0, 1), (1, 0), (1, 1), (2, 0), (2, 1), (3, 0), (3, 1)),
    ((0, 0), (0, 1), (1, 1), (2, 0), (2, 1), (3, 0), (3, 1)),
    ((0, 0), (0, 1), (1, 0), (1, 1), (2, 1), (3, 0), (3, 1)),
    ((2, 0), (2, 1), (0, 0), (0, 1), (1, 0), (1, 1), (3, 1)),
)
TAKES = (
    ((0, 1), (2, 0), (2, 1), (3, 0), (3, 1), (1, 0), (1, 1)),
    ((1, 1), (0, 0), (0, 1), (3, 0), (3, 1), (2, 0), (2, 1)),
    ((2, 1), (1, 0), (3, 0), (3, 1), (0, 0), (0, 1), (1, 1)),
    ((3, 1), (2, 0), (2, 1), (0, 0), (0, 1), (1, 0), (1, 1)),
)


def peers_of(me, table):
    rank, side = me // 2, me % 2
    high, low = rank // 2, rank % 2

    def pick(a, b, c, d):
        return (1 - high) * ((1 - low) * a + low * b) + high * ((1 - low) * c + low * d)

    found = []
    for step in zip(*table):
        other = pick(*(entry[1] for entry in step))
        found.append(2 * pick(*(entry[0] for entry in step)) + side + other - 2 * side * other)
    return found


def fused(
    scale,
    prompt_hbm,
    cache_hbm,
    query_hbm,
    fresh_hbm,
    plen_ref,
    assign_ref,
    ctx_ref,
    out_ref,
    prompt_v,
    cache_v,
    query_v,
    fresh_v,
    fresh_keys,
    query_rope,
    send,
    recv,
    acc,
    top,
    total,
    load_sem,
    prompt_sem,
    send_sem,
    recv_sem,
    relay_sem,
    relayed_sem,
    ready,
):
    me = lax.axis_index("row")
    core = lax.axis_index("tp")
    mate = 1 - core
    targets, sources = peers_of(me, SENDS), peers_of(me, TAKES)
    peers = len(targets) + 1
    rows = cache_v.shape[0]
    cache_len = cache_v.shape[2]
    steps, _, heads, width = query_v.shape
    rope = width - KV_RANK
    piece = prompt_v.shape[1]
    block = 2 * piece
    lanes = rows * rope
    queries_n = steps * heads

    loads = [
        pltpu.make_async_copy(source, target, load_sem.at[i])
        for i, (source, target) in enumerate(
            (
                (query_hbm, query_v),
                (cache_hbm, cache_v),
                (fresh_hbm, fresh_v),
            )
        )
    ]
    groups = prompt_v.shape[0] // 4
    prompt_loads = [
        pltpu.make_async_copy(
            prompt_hbm.at[pl.ds(i * groups, groups)],
            prompt_v.at[pl.ds(i * groups, groups)],
            prompt_sem.at[i],
        )
        for i in range(4)
    ]
    for load in prompt_loads:
        load.start()

    barrier = pltpu.get_barrier_semaphore()

    def tell(semaphore, row):
        pl.semaphore_signal(semaphore, inc=1, device_id={"row": row}, device_id_type=MESH)

    pl.semaphore_signal(barrier, inc=1, device_id={"tp": mate}, device_id_type=MESH)
    for row in range(1, peers):

        @pl.when(row > me)
        def _():
            tell(barrier, row)

    pl.semaphore_wait(barrier, me + 1)
    for row in range(peers - 1):

        @pl.when(row < me)
        def _():
            tell(ready.at[me], row)

    for load in prompt_loads:
        load.wait()

    def pack(dest, target):
        tails = []
        for i in range(rows):
            taken = prompt_v[assign_ref[dest * rows + i]]
            target[:, i * KV_RANK : (i + 1) * KV_RANK] = taken[:, :KV_RANK]
            tails.append(taken[:, KV_RANK:])
        target[:, rows * KV_RANK :] = jnp.concatenate(tails, axis=1)

    early = piece * 3 // 4
    cuts = [pl.ds(0, early), pl.ds(early, piece - early)]
    whole = pl.ds(0, piece)

    def copy_to(step, target, source, cut):
        return pltpu.make_async_remote_copy(
            src_ref=send.at[step, cuts[cut]],
            dst_ref=recv.at[source, core, cuts[cut]],
            send_sem=send_sem.at[step, cut],
            recv_sem=recv_sem.at[source, cut],
            device_id={"row": target},
            device_id_type=MESH,
        )

    def relay_of(step, source, part):
        return pltpu.make_async_remote_copy(
            src_ref=recv.at[source, core, part],
            dst_ref=recv.at[source, core, part],
            send_sem=relay_sem.at[step],
            recv_sem=relayed_sem.at[step],
            device_id={"tp": mate},
            device_id_type=MESH,
        )

    sends = []
    for step, target in enumerate(targets):
        pack(target, send.at[step])

        @pl.when(target > me)
        def _():
            pl.semaphore_wait(ready.at[target], 1)

        for cut in range(2):
            copy = copy_to(step, target, me, cut)
            copy.start()
            sends.append(copy)
    for load in loads:
        load.start()
    arrivals = [[copy_to(step, source, source, cut) for cut in range(2)] for step, source in enumerate(sources)]
    relays = [relay_of(step, source, whole) for step, source in enumerate(sources[:-1])]
    relays += [relay_of(peers - 2 + cut, sources[-1], cuts[cut]) for cut in range(2)]
    own_relay = relay_of(peers, me, whole)
    pack(me, recv.at[me, core])
    own_relay.start()
    fresh_keys[...] = jnp.zeros_like(fresh_keys)
    query_rope[...] = jnp.zeros_like(query_rope)

    for load in loads:
        load.wait()
    nt = (((1,), (1,)), ((), ()))

    def dot_nt(a, b):
        return lax.dot_general(a, b, nt, preferred_element_type=jnp.float32)

    def dot_nn(a, b):
        return jnp.dot(a, b, preferred_element_type=jnp.float32)

    def wide(x):
        return jnp.concatenate([x] * (KV_RANK // lanes), axis=1)

    col = lax.broadcasted_iota(jnp.int32, (queries_n, lanes), 1)
    step_of = lax.broadcasted_iota(jnp.int32, (queries_n, lanes), 0) // heads
    live = [plen_ref[assign_ref[me * rows + i]] for i in range(rows)]
    for i in range(rows):
        q = query_v[:, i].reshape(queries_n, width)
        q_nope, q_rope = q[:, :KV_RANK], q[:, KV_RANK:]
        query_rope[i, :, i * rope : (i + 1) * rope] = q_rope
        fresh_keys[i, :steps, :] = fresh_v[:, i, :]
        ctx = ctx_ref[i]
        parts = []
        values = []
        for first in range(0, cache_len, lanes):
            keys = cache_v[i, :, first : first + lanes]
            s = dot_nn(q_nope, keys[:KV_RANK]) + dot_nn(q_rope, keys[KV_RANK:])
            parts.append(jnp.where(col + first < ctx, s * scale, -jnp.inf))
            values.append(keys[:KV_RANK])
        keys = fresh_keys[i]
        s = dot_nt(q_nope, keys[:, :KV_RANK]) + dot_nt(q_rope, keys[:, KV_RANK:])
        parts.append(jnp.where(col <= step_of, s * scale, -jnp.inf))
        peak = parts[0]
        for s in parts[1:]:
            peak = jnp.maximum(peak, s)
        peak = jnp.broadcast_to(jnp.max(peak, axis=1, keepdims=True), (queries_n, lanes))
        top[i] = peak
        weights = [jnp.exp(s - peak) for s in parts]
        total[i] = sum(weights[1:], weights[0])
        out = dot_nn(weights[-1].astype(jnp.bfloat16), keys[:, :KV_RANK])
        for w, v in zip(weights, values):
            out = out + dot_nt(w.astype(jnp.bfloat16), v)
        acc[i] = out

    def take_in(source):
        limit = source * block
        for i in range(rows):
            keys = recv[source].reshape(block, rows * KV_RANK + lanes)
            q_nope = query_v[:, i].reshape(queries_n, width)[:, :KV_RANK]
            v = keys[:, i * KV_RANK : (i + 1) * KV_RANK]
            s = dot_nt(q_nope, v) + dot_nt(query_rope[i], keys[:, rows * KV_RANK :])
            s = jnp.where(col < live[i] - limit, s * scale, -jnp.inf)
            old = top[i]
            peak = jnp.maximum(old, jnp.max(s, axis=1, keepdims=True))
            shrink = jnp.exp(old - peak)
            w = jnp.exp(s - peak)
            top[i] = peak
            total[i] = total[i] * shrink + w
            acc[i] = acc[i] * wide(shrink) + dot_nn(w.astype(jnp.bfloat16), v)

    def take_half(source, half, last):
        limit = source * block + half * piece
        for i in range(rows):
            keys = recv[source, half]
            q_nope = query_v[:, i].reshape(queries_n, width)[:, :KV_RANK]
            v = keys[:, i * KV_RANK : (i + 1) * KV_RANK]
            s = dot_nt(q_nope, v) + dot_nt(query_rope[i], keys[:, rows * KV_RANK :])
            s = jnp.where(col[:, :piece] < live[i] - limit, s * scale, -jnp.inf)
            old = top[i]
            peak = jnp.maximum(old, jnp.max(s, axis=1, keepdims=True))
            shrink = jnp.exp(old - peak)
            w = jnp.exp(s - peak[:, :piece])
            mixed = acc[i] * wide(shrink) + dot_nn(w.astype(jnp.bfloat16), v)
            if last:
                mass = jnp.sum(total[i] * shrink, axis=1, keepdims=True)
                mass = mass + jnp.sum(w, axis=1, keepdims=True)
                mixed = (mixed * (1.0 / mass)).astype(out_ref.dtype)
                out_ref[:, i] = mixed.reshape(steps, heads, KV_RANK)
            else:
                top[i] = peak
                total[i] = total[i] * shrink
                total[i, :, :piece] += w
                acc[i] = mixed

    own_relay.wait_recv()
    take_in(me)
    for step in range(peers - 2):
        for arrival in arrivals[step]:
            arrival.wait_recv()
        relays[step].start()
        if step:
            relays[step - 1].wait_recv()
            take_in(sources[step - 1])
    relays[peers - 3].wait_recv()
    take_in(sources[-2])
    for arrival, relay in zip(arrivals[-1], relays[-2:]):
        arrival.wait_recv()
        relay.start()
    take_half(sources[-1], core, False)
    for relay in relays[-2:]:
        relay.wait_recv()
    take_half(sources[-1], mate, True)
    for copy in sends:
        copy.wait_send()
    for relay in relays + [own_relay]:
        relay.wait_send()


def direct(prompt_latent, row_cache, queries, new_latent, prompt_len, assign, row_ctx):
    peers = lax.axis_size("row")
    steps, rows, heads, width = queries.shape
    rope = width - KV_RANK
    local = prompt_latent.reshape(prompt_latent.shape[1:])
    cache_t = jnp.swapaxes(row_cache, 1, 2)
    piece = local.shape[1]
    lanes = rows * rope
    packed = rows * KV_RANK + lanes
    total_n = steps * heads
    bf16, f32 = jnp.bfloat16, jnp.float32
    hbm = pl.BlockSpec(memory_space=pl.ANY)
    smem = pl.BlockSpec(memory_space=pltpu.SMEM)
    return pl.pallas_call(
        functools.partial(fused, (NOPE_DIM + ROPE_DIM) ** (-0.5)),
        out_shape=pltpu.VMEM((steps, rows, heads, KV_RANK), bf16),
        in_specs=[hbm, hbm, hbm, hbm, smem, smem, smem],
        out_specs=pl.BlockSpec(memory_space=pltpu.VMEM),
        scratch_shapes=[
            pltpu.VMEM(local.shape, bf16),
            pltpu.VMEM(cache_t.shape, bf16),
            pltpu.VMEM(queries.shape, bf16),
            pltpu.VMEM(new_latent.shape, bf16),
            pltpu.VMEM((rows, lanes, width), bf16),
            pltpu.VMEM((rows, total_n, lanes), bf16),
            pltpu.VMEM((peers - 1, piece, packed), bf16),
            pltpu.VMEM((peers, 2, piece, packed), bf16),
            pltpu.VMEM((rows, total_n, KV_RANK), f32),
            pltpu.VMEM((rows, total_n, lanes), f32),
            pltpu.VMEM((rows, total_n, lanes), f32),
            pltpu.SemaphoreType.DMA((3,)),
            pltpu.SemaphoreType.DMA((4,)),
            pltpu.SemaphoreType.DMA((peers - 1, 2)),
            pltpu.SemaphoreType.DMA((peers, 2)),
            pltpu.SemaphoreType.DMA((peers + 1,)),
            pltpu.SemaphoreType.DMA((peers + 1,)),
            pltpu.SemaphoreType.REGULAR((peers,)),
        ],
        compiler_params=pltpu.CompilerParams(collective_id=0, has_side_effects=True),
    )(local, cache_t, queries, new_latent, prompt_len, assign, row_ctx)


def solution(mesh):
    one_group = mesh.shape["row"] == SPR and mesh.shape["tp"] == 2
    return jax.shard_map(
        direct if one_group else shards,
        mesh=mesh,
        in_specs=(
            P(("group", "row"), None, "tp", None),
            P(("group", "row"), None, None),
            P(None, ("group", "row"), "tp", None),
            P(None, ("group", "row"), None),
            P("group"),
            P("group"),
            P(("group", "row")),
        ),
        out_specs=P(None, ("group", "row"), "tp", None),
        check_vma=False,
    )
```

```python
import functools

import jax
import jax.numpy as jnp
from jax import lax
from jax.experimental import pallas as pl
from jax.experimental.pallas import tpu as pltpu
from jax.sharding import PartitionSpec as P

KV_RANK = 512
ROPE_DIM = 64
NOPE_DIM = 128
SPR = 8


def pick(array, index):
    return lax.map(lambda i: lax.dynamic_index_in_dim(array, i, 0, keepdims=False), index)


def shards(prompt_latent, row_cache, queries, new_latent, prompt_len, assign, row_ctx):
    row_count = lax.axis_size("row")
    pair_count = lax.axis_size("tp")
    row_place = lax.axis_index("row")
    rows_here = row_cache.shape[0]
    group_rows = prompt_latent.shape[1]
    piece_len = prompt_latent.shape[2]
    latent_width = prompt_latent.shape[3]
    full_len = piece_len * SPR * pair_count
    most_slots = min(rows_here, max(2, 2 * rows_here * SPR // row_count))
    home_group = row_place // SPR
    dest_prompt = assign.reshape(row_count, rows_here)
    in_group = dest_prompt // group_rows == home_group
    row_ids = jnp.arange(rows_here, dtype=jnp.int32)
    up_to = row_ids[:, None] <= row_ids[None, :]
    rank = jnp.sum((in_group[:, :, None] & up_to[None]).astype(jnp.int32), axis=1) - 1
    slot_ids = jnp.arange(most_slots, dtype=jnp.int32)
    picked = in_group[:, :, None] & (rank[:, :, None] == slot_ids[None, None, :])
    local_id = dest_prompt - home_group * group_rows
    source_index = jnp.sum(jnp.where(picked, local_id[:, :, None], 0), axis=1)
    filled = jnp.any(picked, axis=1).reshape(-1)
    owned = lax.dynamic_slice_in_dim(assign, row_place * rows_here, rows_here)
    owned_group = owned // group_rows
    same_before = (owned_group[:, None] == owned_group[None, :]) & (
        row_ids[None, :] < row_ids[:, None]
    )
    own_rank = jnp.sum(same_before.astype(jnp.int32), axis=1)
    block_ids = jnp.arange(SPR, dtype=jnp.int32)
    fetch_index = (
        (owned_group[:, None] * SPR + block_ids[None, :]) * most_slots + own_rank[:, None]
    ).reshape(-1)
    local = prompt_latent[0]
    rows_taken = pick(local, source_index.reshape(-1))
    rows_taken = jnp.where(filled[:, None, None], rows_taken, jnp.zeros_like(rows_taken))
    moved = lax.all_to_all(
        rows_taken.reshape((row_count, most_slots) + local.shape[1:]),
        "row",
        split_axis=0,
        concat_axis=0,
        tiled=True,
    )
    flat = moved.reshape(row_count * most_slots, piece_len, latent_width)
    mine = pick(flat, fetch_index).reshape(rows_here, SPR, 1, piece_len, latent_width)
    paired = lax.all_gather(mine, "tp", axis=2, tiled=True)
    latents = paired.reshape(rows_here, full_len, latent_width)
    live_len = pick(prompt_len, owned)
    scale_factor = (NOPE_DIM + ROPE_DIM) ** (-0.5)
    steps_count = queries.shape[0]
    cache_len = row_cache.shape[1]
    cache_scores = (
        jnp.einsum("srhc,rkc->rshk", queries, row_cache, preferred_element_type=jnp.float32)
        * scale_factor
    )
    cache_live = jnp.arange(cache_len, dtype=jnp.int32)[None, :] < row_ctx[:, None]
    cache_scores = jnp.where(cache_live[:, None, None, :], cache_scores, -jnp.inf)
    fresh_scores = (
        jnp.einsum("srhc,jrc->rshj", queries, new_latent, preferred_element_type=jnp.float32)
        * scale_factor
    )
    step_ids = jnp.arange(steps_count, dtype=jnp.int32)
    causal = step_ids[None, :] <= step_ids[:, None]
    fresh_scores = jnp.where(causal[None, :, None, :], fresh_scores, -jnp.inf)
    prompt_live = jnp.arange(full_len, dtype=jnp.int32)[None, :] < live_len[:, None]
    prompt_scores = (
        jnp.einsum("srhc,rkc->rshk", queries, latents, preferred_element_type=jnp.float32)
        * scale_factor
    )
    prompt_scores = jnp.where(prompt_live[:, None, None, :], prompt_scores, -jnp.inf)
    row_top = jnp.maximum(
        jnp.max(prompt_scores, axis=3, keepdims=True),
        jnp.maximum(
            jnp.max(cache_scores, axis=3, keepdims=True),
            jnp.max(fresh_scores, axis=3, keepdims=True),
        ),
    )
    prompt_exp = jnp.exp(prompt_scores - row_top)
    cache_exp = jnp.exp(cache_scores - row_top)
    fresh_exp = jnp.exp(fresh_scores - row_top)
    denominator = (
        jnp.sum(prompt_exp, axis=3, keepdims=True)
        + jnp.sum(cache_exp, axis=3, keepdims=True)
        + jnp.sum(fresh_exp, axis=3, keepdims=True)
    )
    prompt_probs = (prompt_exp / denominator).astype(jnp.bfloat16)
    cache_probs = (cache_exp / denominator).astype(jnp.bfloat16)
    fresh_probs = (fresh_exp / denominator).astype(jnp.bfloat16)
    cache_out = jnp.einsum(
        "rshk,rkc->srhc", cache_probs, row_cache[:, :, :KV_RANK], preferred_element_type=jnp.float32
    )
    fresh_out = jnp.einsum(
        "rshj,jrc->srhc",
        fresh_probs,
        new_latent[:, :, :KV_RANK],
        preferred_element_type=jnp.float32,
    )
    prompt_out = jnp.einsum(
        "rshk,rkc->srhc", prompt_probs, latents[:, :, :KV_RANK], preferred_element_type=jnp.float32
    )
    return (prompt_out + cache_out + fresh_out).astype(jnp.bfloat16)


MESH = pl.DeviceIdType.MESH


TAKES = (
    ((3, 0), (3, 1), (0, 1), (1, 0), (1, 1), (2, 0), (2, 1)),
    ((1, 1), (0, 0), (0, 1), (3, 0), (3, 1), (2, 0), (2, 1)),
    ((2, 1), (0, 0), (0, 1), (3, 0), (3, 1), (1, 0), (1, 1)),
    ((3, 1), (2, 0), (2, 1), (0, 0), (0, 1), (1, 0), (1, 1)),
)


def peers_of(me, table):
    rank, side = me // 2, me % 2
    high, low = rank // 2, rank % 2

    def pick(a, b, c, d):
        return (1 - high) * ((1 - low) * a + low * b) + high * ((1 - low) * c + low * d)

    found = []
    for step in zip(*table):
        other = pick(*(entry[1] for entry in step))
        found.append(2 * pick(*(entry[0] for entry in step)) + side + other - 2 * side * other)
    return found


def fused(
    scale,
    prompt_hbm,
    cache_hbm,
    query_hbm,
    fresh_hbm,
    plen_ref,
    assign_ref,
    ctx_ref,
    out_ref,
    prompt_v,
    cache_v,
    query_v,
    fresh_v,
    fresh_keys,
    query_rope,
    send,
    recv,
    acc,
    top,
    total,
    load_sem,
    prompt_sem,
    send_sem,
    recv_sem,
    relay_sem,
    relayed_sem,
    ready,
):
    me = lax.axis_index("row")
    core = lax.axis_index("tp")
    mate = 1 - core
    sources = peers_of(me, TAKES)
    targets = [row + (me <= row).astype(jnp.int32) for row in range(len(sources))]
    peers = len(targets) + 1
    rows = cache_v.shape[0]
    cache_len = cache_v.shape[2]
    steps, _, heads, width = query_v.shape
    rope = width - KV_RANK
    piece = prompt_v.shape[1]
    block = 2 * piece
    lanes = rows * rope
    queries_n = steps * heads

    loads = [
        pltpu.make_async_copy(source, target, load_sem.at[i])
        for i, (source, target) in enumerate(
            (
                (query_hbm, query_v),
                (cache_hbm, cache_v),
                (fresh_hbm, fresh_v),
            )
        )
    ]
    groups = prompt_v.shape[0] // 4
    prompt_loads = [
        pltpu.make_async_copy(
            prompt_hbm.at[pl.ds(i * groups, groups)],
            prompt_v.at[pl.ds(i * groups, groups)],
            prompt_sem.at[i],
        )
        for i in range(4)
    ]
    for load in prompt_loads:
        load.start()

    barrier = pltpu.get_barrier_semaphore()

    def tell(semaphore, row):
        pl.semaphore_signal(semaphore, inc=1, device_id={"row": row}, device_id_type=MESH)

    pl.semaphore_signal(barrier, inc=1, device_id={"tp": mate}, device_id_type=MESH)
    for row in range(1, peers):

        @pl.when(row > me)
        def _():
            tell(barrier, row)

    pl.semaphore_wait(barrier, me + 1)
    for row in range(peers - 1):

        @pl.when(row < me)
        def _():
            tell(ready.at[me], row)

    for load in prompt_loads:
        load.wait()

    def pack(dest, target):
        tails = []
        for i in range(rows):
            taken = prompt_v[assign_ref[dest * rows + i]]
            target[:, i * KV_RANK : (i + 1) * KV_RANK] = taken[:, :KV_RANK]
            tails.append(taken[:, KV_RANK:])
        target[:, rows * KV_RANK :] = jnp.concatenate(tails, axis=1)

    early = piece * 3 // 4
    cuts = [pl.ds(0, early), pl.ds(early, piece - early)]
    whole = pl.ds(0, piece)

    def copy_to(step, target, source, cut):
        return pltpu.make_async_remote_copy(
            src_ref=send.at[step, cuts[cut]],
            dst_ref=recv.at[source, core, cuts[cut]],
            send_sem=send_sem.at[step, cut],
            recv_sem=recv_sem.at[source, cut],
            device_id={"row": target},
            device_id_type=MESH,
        )

    def relay_of(step, source, part):
        return pltpu.make_async_remote_copy(
            src_ref=recv.at[source, core, part],
            dst_ref=recv.at[source, core, part],
            send_sem=relay_sem.at[step],
            recv_sem=relayed_sem.at[step],
            device_id={"tp": mate},
            device_id_type=MESH,
        )

    sends = []
    for step, target in enumerate(targets):
        pack(target, send.at[step])

        @pl.when(target > me)
        def _():
            pl.semaphore_wait(ready.at[target], 1)

        for cut in range(2):
            copy = copy_to(step, target, me, cut)
            copy.start()
            sends.append(copy)
    for load in loads:
        load.start()
    arrivals = [[copy_to(step, source, source, cut) for cut in range(2)] for step, source in enumerate(sources)]
    relays = [relay_of(step, source, whole) for step, source in enumerate(sources[:-1])]
    relays += [relay_of(peers - 2 + cut, sources[-1], cuts[cut]) for cut in range(2)]
    own_relay = relay_of(peers, me, whole)
    pack(me, recv.at[me, core])
    own_relay.start()
    fresh_keys[...] = jnp.zeros_like(fresh_keys)
    query_rope[...] = jnp.zeros_like(query_rope)

    for load in loads:
        load.wait()
    nt = (((1,), (1,)), ((), ()))

    def dot_nt(a, b):
        return lax.dot_general(a, b, nt, preferred_element_type=jnp.float32)

    def dot_nn(a, b):
        return jnp.dot(a, b, preferred_element_type=jnp.float32)

    def wide(x):
        return jnp.concatenate([x] * (KV_RANK // lanes), axis=1)

    col = lax.broadcasted_iota(jnp.int32, (queries_n, lanes), 1)
    step_of = lax.broadcasted_iota(jnp.int32, (queries_n, lanes), 0) // heads
    live = [plen_ref[assign_ref[me * rows + i]] for i in range(rows)]
    for i in range(rows):
        q = query_v[:, i].reshape(queries_n, width)
        q_nope, q_rope = q[:, :KV_RANK], q[:, KV_RANK:]
        query_rope[i, :, i * rope : (i + 1) * rope] = q_rope
        fresh_keys[i, :steps, :] = fresh_v[:, i, :]
        ctx = ctx_ref[i]
        parts = []
        values = []
        for first in range(0, cache_len, lanes):
            keys = cache_v[i, :, first : first + lanes]
            s = dot_nn(q_nope, keys[:KV_RANK]) + dot_nn(q_rope, keys[KV_RANK:])
            parts.append(jnp.where(col + first < ctx, s * scale, -jnp.inf))
            values.append(keys[:KV_RANK])
        keys = fresh_keys[i]
        s = dot_nt(q_nope, keys[:, :KV_RANK]) + dot_nt(q_rope, keys[:, KV_RANK:])
        parts.append(jnp.where(col <= step_of, s * scale, -jnp.inf))
        peak = parts[0]
        for s in parts[1:]:
            peak = jnp.maximum(peak, s)
        peak = jnp.broadcast_to(jnp.max(peak, axis=1, keepdims=True), (queries_n, lanes))
        top[i] = peak
        weights = [jnp.exp(s - peak) for s in parts]
        total[i] = sum(weights[1:], weights[0])
        out = dot_nn(weights[-1].astype(jnp.bfloat16), keys[:, :KV_RANK])
        for w, v in zip(weights, values):
            out = out + dot_nt(w.astype(jnp.bfloat16), v)
        acc[i] = out

    def take_in(source):
        limit = source * block
        for i in range(rows):
            keys = recv[source].reshape(block, rows * KV_RANK + lanes)
            q_nope = query_v[:, i].reshape(queries_n, width)[:, :KV_RANK]
            v = keys[:, i * KV_RANK : (i + 1) * KV_RANK]
            s = dot_nt(q_nope, v) + dot_nt(query_rope[i], keys[:, rows * KV_RANK :])
            s = jnp.where(col < live[i] - limit, s * scale, -jnp.inf)
            old = top[i]
            peak = jnp.maximum(old, jnp.max(s, axis=1, keepdims=True))
            shrink = jnp.exp(old - peak)
            w = jnp.exp(s - peak)
            top[i] = peak
            total[i] = total[i] * shrink + w
            acc[i] = acc[i] * wide(shrink) + dot_nn(w.astype(jnp.bfloat16), v)

    def take_half(source, half, last):
        limit = source * block + half * piece
        for i in range(rows):
            keys = recv[source, half]
            q_nope = query_v[:, i].reshape(queries_n, width)[:, :KV_RANK]
            v = keys[:, i * KV_RANK : (i + 1) * KV_RANK]
            s = dot_nt(q_nope, v) + dot_nt(query_rope[i], keys[:, rows * KV_RANK :])
            s = jnp.where(col[:, :piece] < live[i] - limit, s * scale, -jnp.inf)
            old = top[i]
            peak = jnp.maximum(old, jnp.max(s, axis=1, keepdims=True))
            shrink = jnp.exp(old - peak)
            w = jnp.exp(s - peak[:, :piece])
            mixed = acc[i] * wide(shrink) + dot_nn(w.astype(jnp.bfloat16), v)
            if last:
                mass = jnp.sum(total[i] * shrink, axis=1, keepdims=True)
                mass = mass + jnp.sum(w, axis=1, keepdims=True)
                mixed = (mixed * (1.0 / mass)).astype(out_ref.dtype)
                out_ref[:, i] = mixed.reshape(steps, heads, KV_RANK)
            else:
                top[i] = peak
                total[i] = total[i] * shrink
                total[i, :, :piece] += w
                acc[i] = mixed

    own_relay.wait_recv()
    take_in(me)
    for step in range(peers - 2):
        for arrival in arrivals[step]:
            arrival.wait_recv()
        relays[step].start()
        if step:
            relays[step - 1].wait_recv()
            take_in(sources[step - 1])
    relays[peers - 3].wait_recv()
    take_in(sources[-2])
    for arrival, relay in zip(arrivals[-1], relays[-2:]):
        arrival.wait_recv()
        relay.start()
    take_half(sources[-1], core, False)
    for relay in relays[-2:]:
        relay.wait_recv()
    take_half(sources[-1], mate, True)
    for copy in sends:
        copy.wait_send()
    for relay in relays + [own_relay]:
        relay.wait_send()


def direct(prompt_latent, row_cache, queries, new_latent, prompt_len, assign, row_ctx):
    peers = lax.axis_size("row")
    steps, rows, heads, width = queries.shape
    rope = width - KV_RANK
    local = prompt_latent.reshape(prompt_latent.shape[1:])
    cache_t = jnp.swapaxes(row_cache, 1, 2)
    piece = local.shape[1]
    lanes = rows * rope
    packed = rows * KV_RANK + lanes
    total_n = steps * heads
    bf16, f32 = jnp.bfloat16, jnp.float32
    hbm = pl.BlockSpec(memory_space=pl.ANY)
    smem = pl.BlockSpec(memory_space=pltpu.SMEM)
    return pl.pallas_call(
        functools.partial(fused, (NOPE_DIM + ROPE_DIM) ** (-0.5)),
        out_shape=pltpu.VMEM((steps, rows, heads, KV_RANK), bf16),
        in_specs=[hbm, hbm, hbm, hbm, smem, smem, smem],
        out_specs=pl.BlockSpec(memory_space=pltpu.VMEM),
        scratch_shapes=[
            pltpu.VMEM(local.shape, bf16),
            pltpu.VMEM(cache_t.shape, bf16),
            pltpu.VMEM(queries.shape, bf16),
            pltpu.VMEM(new_latent.shape, bf16),
            pltpu.VMEM((rows, lanes, width), bf16),
            pltpu.VMEM((rows, total_n, lanes), bf16),
            pltpu.VMEM((peers - 1, piece, packed), bf16),
            pltpu.VMEM((peers, 2, piece, packed), bf16),
            pltpu.VMEM((rows, total_n, KV_RANK), f32),
            pltpu.VMEM((rows, total_n, lanes), f32),
            pltpu.VMEM((rows, total_n, lanes), f32),
            pltpu.SemaphoreType.DMA((3,)),
            pltpu.SemaphoreType.DMA((4,)),
            pltpu.SemaphoreType.DMA((peers - 1, 2)),
            pltpu.SemaphoreType.DMA((peers, 2)),
            pltpu.SemaphoreType.DMA((peers + 1,)),
            pltpu.SemaphoreType.DMA((peers + 1,)),
            pltpu.SemaphoreType.REGULAR((peers,)),
        ],
        compiler_params=pltpu.CompilerParams(collective_id=0, has_side_effects=True),
    )(local, cache_t, queries, new_latent, prompt_len, assign, row_ctx)


def solution(mesh):
    one_group = mesh.shape["row"] == SPR and mesh.shape["tp"] == 2
    return jax.shard_map(
        direct if one_group else shards,
        mesh=mesh,
        in_specs=(
            P(("group", "row"), None, "tp", None),
            P(("group", "row"), None, None),
            P(None, ("group", "row"), "tp", None),
            P(None, ("group", "row"), None),
            P("group"),
            P("group"),
            P(("group", "row")),
        ),
        out_specs=P(None, ("group", "row"), "tp", None),
        check_vma=False,
    )
```

```python
import functools

import jax
import jax.numpy as jnp
from jax import lax
from jax.experimental import pallas as pl
from jax.experimental.pallas import tpu as pltpu
from jax.sharding import PartitionSpec as P

KV_RANK = 512
ROPE_DIM = 64
NOPE_DIM = 128
SPR = 8


def pick(array, index):
    return lax.map(lambda i: lax.dynamic_index_in_dim(array, i, 0, keepdims=False), index)


def shards(prompt_latent, row_cache, queries, new_latent, prompt_len, assign, row_ctx):
    row_count = lax.axis_size("row")
    pair_count = lax.axis_size("tp")
    row_place = lax.axis_index("row")
    rows_here = row_cache.shape[0]
    group_rows = prompt_latent.shape[1]
    piece_len = prompt_latent.shape[2]
    latent_width = prompt_latent.shape[3]
    full_len = piece_len * SPR * pair_count
    most_slots = min(rows_here, max(2, 2 * rows_here * SPR // row_count))
    home_group = row_place // SPR
    dest_prompt = assign.reshape(row_count, rows_here)
    in_group = dest_prompt // group_rows == home_group
    row_ids = jnp.arange(rows_here, dtype=jnp.int32)
    up_to = row_ids[:, None] <= row_ids[None, :]
    rank = jnp.sum((in_group[:, :, None] & up_to[None]).astype(jnp.int32), axis=1) - 1
    slot_ids = jnp.arange(most_slots, dtype=jnp.int32)
    picked = in_group[:, :, None] & (rank[:, :, None] == slot_ids[None, None, :])
    local_id = dest_prompt - home_group * group_rows
    source_index = jnp.sum(jnp.where(picked, local_id[:, :, None], 0), axis=1)
    filled = jnp.any(picked, axis=1).reshape(-1)
    owned = lax.dynamic_slice_in_dim(assign, row_place * rows_here, rows_here)
    owned_group = owned // group_rows
    same_before = (owned_group[:, None] == owned_group[None, :]) & (
        row_ids[None, :] < row_ids[:, None]
    )
    own_rank = jnp.sum(same_before.astype(jnp.int32), axis=1)
    block_ids = jnp.arange(SPR, dtype=jnp.int32)
    fetch_index = (
        (owned_group[:, None] * SPR + block_ids[None, :]) * most_slots + own_rank[:, None]
    ).reshape(-1)
    local = prompt_latent[0]
    rows_taken = pick(local, source_index.reshape(-1))
    rows_taken = jnp.where(filled[:, None, None], rows_taken, jnp.zeros_like(rows_taken))
    moved = lax.all_to_all(
        rows_taken.reshape((row_count, most_slots) + local.shape[1:]),
        "row",
        split_axis=0,
        concat_axis=0,
        tiled=True,
    )
    flat = moved.reshape(row_count * most_slots, piece_len, latent_width)
    mine = pick(flat, fetch_index).reshape(rows_here, SPR, 1, piece_len, latent_width)
    paired = lax.all_gather(mine, "tp", axis=2, tiled=True)
    latents = paired.reshape(rows_here, full_len, latent_width)
    live_len = pick(prompt_len, owned)
    scale_factor = (NOPE_DIM + ROPE_DIM) ** (-0.5)
    steps_count = queries.shape[0]
    cache_len = row_cache.shape[1]
    cache_scores = (
        jnp.einsum("srhc,rkc->rshk", queries, row_cache, preferred_element_type=jnp.float32)
        * scale_factor
    )
    cache_live = jnp.arange(cache_len, dtype=jnp.int32)[None, :] < row_ctx[:, None]
    cache_scores = jnp.where(cache_live[:, None, None, :], cache_scores, -jnp.inf)
    fresh_scores = (
        jnp.einsum("srhc,jrc->rshj", queries, new_latent, preferred_element_type=jnp.float32)
        * scale_factor
    )
    step_ids = jnp.arange(steps_count, dtype=jnp.int32)
    causal = step_ids[None, :] <= step_ids[:, None]
    fresh_scores = jnp.where(causal[None, :, None, :], fresh_scores, -jnp.inf)
    prompt_live = jnp.arange(full_len, dtype=jnp.int32)[None, :] < live_len[:, None]
    prompt_scores = (
        jnp.einsum("srhc,rkc->rshk", queries, latents, preferred_element_type=jnp.float32)
        * scale_factor
    )
    prompt_scores = jnp.where(prompt_live[:, None, None, :], prompt_scores, -jnp.inf)
    row_top = jnp.maximum(
        jnp.max(prompt_scores, axis=3, keepdims=True),
        jnp.maximum(
            jnp.max(cache_scores, axis=3, keepdims=True),
            jnp.max(fresh_scores, axis=3, keepdims=True),
        ),
    )
    prompt_exp = jnp.exp(prompt_scores - row_top)
    cache_exp = jnp.exp(cache_scores - row_top)
    fresh_exp = jnp.exp(fresh_scores - row_top)
    denominator = (
        jnp.sum(prompt_exp, axis=3, keepdims=True)
        + jnp.sum(cache_exp, axis=3, keepdims=True)
        + jnp.sum(fresh_exp, axis=3, keepdims=True)
    )
    prompt_probs = (prompt_exp / denominator).astype(jnp.bfloat16)
    cache_probs = (cache_exp / denominator).astype(jnp.bfloat16)
    fresh_probs = (fresh_exp / denominator).astype(jnp.bfloat16)
    cache_out = jnp.einsum(
        "rshk,rkc->srhc", cache_probs, row_cache[:, :, :KV_RANK], preferred_element_type=jnp.float32
    )
    fresh_out = jnp.einsum(
        "rshj,jrc->srhc",
        fresh_probs,
        new_latent[:, :, :KV_RANK],
        preferred_element_type=jnp.float32,
    )
    prompt_out = jnp.einsum(
        "rshk,rkc->srhc", prompt_probs, latents[:, :, :KV_RANK], preferred_element_type=jnp.float32
    )
    return (prompt_out + cache_out + fresh_out).astype(jnp.bfloat16)


MESH = pl.DeviceIdType.MESH


LEVELS = (1, 0, 0, 2)
SENDS = (
    ((2, 0), (2, 1), (1, 0), (1, 1), (0, 1), (3, 0), (3, 1)),
    ((2, 0), (2, 1), (1, 1), (0, 0), (0, 1), (3, 0), (3, 1)),
    ((1, 0), (0, 0), (0, 1), (1, 1), (2, 1), (3, 0), (3, 1)),
    ((1, 0), (1, 1), (2, 0), (2, 1), (0, 0), (0, 1), (3, 1)),
)
TAKES = (
    ((0, 1), (1, 0), (1, 1), (2, 0), (3, 0), (3, 1), (2, 1)),
    ((1, 1), (3, 0), (3, 1), (2, 0), (0, 0), (0, 1), (2, 1)),
    ((0, 0), (0, 1), (2, 1), (1, 0), (3, 0), (3, 1), (1, 1)),
    ((3, 1), (2, 0), (2, 1), (0, 0), (0, 1), (1, 0), (1, 1)),
)


def by_rank(rank, a, b, c, d):
    high, low = rank // 2, rank % 2
    return (1 - high) * ((1 - low) * a + low * b) + high * ((1 - low) * c + low * d)


def peers_of(me, table):
    rank, side = me // 2, me % 2
    found = []
    for step in zip(*table):
        other = by_rank(rank, *(entry[1] for entry in step))
        found.append(2 * by_rank(rank, *(entry[0] for entry in step)) + side + other - 2 * side * other)
    return found


def fused(
    scale,
    prompt_hbm,
    cache_hbm,
    query_hbm,
    fresh_hbm,
    plen_ref,
    assign_ref,
    ctx_ref,
    out_ref,
    prompt_v,
    cache_v,
    query_v,
    fresh_v,
    fresh_keys,
    query_rope,
    send,
    recv,
    acc,
    top,
    total,
    load_sem,
    prompt_sem,
    send_sem,
    recv_sem,
    relay_sem,
    relayed_sem,
    ready,
):
    me = lax.axis_index("row")
    core = lax.axis_index("tp")
    mate = 1 - core
    targets, sources = peers_of(me, SENDS), peers_of(me, TAKES)
    peers = len(targets) + 1
    rows = cache_v.shape[0]
    cache_len = cache_v.shape[2]
    steps, _, heads, width = query_v.shape
    rope = width - KV_RANK
    piece = prompt_v.shape[1]
    block = 2 * piece
    lanes = rows * rope
    queries_n = steps * heads

    loads = [
        pltpu.make_async_copy(source, target, load_sem.at[i])
        for i, (source, target) in enumerate(
            (
                (query_hbm, query_v),
                (cache_hbm, cache_v),
                (fresh_hbm, fresh_v),
            )
        )
    ]
    groups = prompt_v.shape[0] // 4
    prompt_loads = [
        pltpu.make_async_copy(
            prompt_hbm.at[pl.ds(i * groups, groups)],
            prompt_v.at[pl.ds(i * groups, groups)],
            prompt_sem.at[i],
        )
        for i in range(4)
    ]
    for load in prompt_loads:
        load.start()

    barrier = pltpu.get_barrier_semaphore()

    def tell(semaphore, row):
        pl.semaphore_signal(semaphore, inc=1, device_id={"row": row}, device_id_type=MESH)

    pl.semaphore_signal(barrier, inc=1, device_id={"tp": mate}, device_id_type=MESH)
    level = by_rank(me // 2, *LEVELS)
    row_levels = [LEVELS[row // 2] for row in range(peers)]
    for row, its in enumerate(row_levels):

        @pl.when((row != me) & (its >= level))
        def _():
            tell(barrier, row)

    pl.semaphore_wait(barrier, by_rank(me // 2, *(sum(its <= LEVELS[r] for its in row_levels) for r in range(4))))
    for row, its in enumerate(row_levels):

        @pl.when(its < level)
        def _():
            tell(ready.at[me], row)

    for load in prompt_loads:
        load.wait()

    def pack(dest, target):
        tails = []
        for i in range(rows):
            taken = prompt_v[assign_ref[dest * rows + i]]
            target[:, i * KV_RANK : (i + 1) * KV_RANK] = taken[:, :KV_RANK]
            tails.append(taken[:, KV_RANK:])
        target[:, rows * KV_RANK :] = jnp.concatenate(tails, axis=1)

    early = piece * 3 // 4
    cuts = [pl.ds(0, early), pl.ds(early, piece - early)]
    whole = pl.ds(0, piece)

    def copy_to(step, target, source, cut):
        return pltpu.make_async_remote_copy(
            src_ref=send.at[step, cuts[cut]],
            dst_ref=recv.at[source, core, cuts[cut]],
            send_sem=send_sem.at[step, cut],
            recv_sem=recv_sem.at[source, cut],
            device_id={"row": target},
            device_id_type=MESH,
        )

    def relay_of(step, source, part):
        return pltpu.make_async_remote_copy(
            src_ref=recv.at[source, core, part],
            dst_ref=recv.at[source, core, part],
            send_sem=relay_sem.at[step],
            recv_sem=relayed_sem.at[step],
            device_id={"tp": mate},
            device_id_type=MESH,
        )

    sends = []
    for step, target in enumerate(targets):
        pack(target, send.at[step])

        @pl.when(by_rank(target // 2, *LEVELS) > level)
        def _():
            pl.semaphore_wait(ready.at[target], 1)

        for cut in range(2):
            copy = copy_to(step, target, me, cut)
            copy.start()
            sends.append(copy)
    for load in loads:
        load.start()
    arrivals = [[copy_to(step, source, source, cut) for cut in range(2)] for step, source in enumerate(sources)]
    relays = [relay_of(step, source, whole) for step, source in enumerate(sources[:-1])]
    relays += [relay_of(peers - 2 + cut, sources[-1], cuts[cut]) for cut in range(2)]
    own_relay = relay_of(peers, me, whole)
    pack(me, recv.at[me, core])
    own_relay.start()
    fresh_keys[...] = jnp.zeros_like(fresh_keys)
    query_rope[...] = jnp.zeros_like(query_rope)

    for load in loads:
        load.wait()
    nt = (((1,), (1,)), ((), ()))

    def dot_nt(a, b):
        return lax.dot_general(a, b, nt, preferred_element_type=jnp.float32)

    def dot_nn(a, b):
        return jnp.dot(a, b, preferred_element_type=jnp.float32)

    def wide(x):
        return jnp.concatenate([x] * (KV_RANK // lanes), axis=1)

    col = lax.broadcasted_iota(jnp.int32, (queries_n, lanes), 1)
    step_of = lax.broadcasted_iota(jnp.int32, (queries_n, lanes), 0) // heads
    live = [plen_ref[assign_ref[me * rows + i]] for i in range(rows)]
    for i in range(rows):
        q = query_v[:, i].reshape(queries_n, width)
        q_nope, q_rope = q[:, :KV_RANK], q[:, KV_RANK:]
        query_rope[i, :, i * rope : (i + 1) * rope] = q_rope
        fresh_keys[i, :steps, :] = fresh_v[:, i, :]
        ctx = ctx_ref[i]
        parts = []
        values = []
        for first in range(0, cache_len, lanes):
            keys = cache_v[i, :, first : first + lanes]
            s = dot_nn(q_nope, keys[:KV_RANK]) + dot_nn(q_rope, keys[KV_RANK:])
            parts.append(jnp.where(col + first < ctx, s * scale, -jnp.inf))
            values.append(keys[:KV_RANK])
        keys = fresh_keys[i]
        s = dot_nt(q_nope, keys[:, :KV_RANK]) + dot_nt(q_rope, keys[:, KV_RANK:])
        parts.append(jnp.where(col <= step_of, s * scale, -jnp.inf))
        peak = parts[0]
        for s in parts[1:]:
            peak = jnp.maximum(peak, s)
        peak = jnp.broadcast_to(jnp.max(peak, axis=1, keepdims=True), (queries_n, lanes))
        top[i] = peak
        weights = [jnp.exp(s - peak) for s in parts]
        total[i] = sum(weights[1:], weights[0])
        out = dot_nn(weights[-1].astype(jnp.bfloat16), keys[:, :KV_RANK])
        for w, v in zip(weights, values):
            out = out + dot_nt(w.astype(jnp.bfloat16), v)
        acc[i] = out

    def take_in(source):
        limit = source * block
        for i in range(rows):
            keys = recv[source].reshape(block, rows * KV_RANK + lanes)
            q_nope = query_v[:, i].reshape(queries_n, width)[:, :KV_RANK]
            v = keys[:, i * KV_RANK : (i + 1) * KV_RANK]
            s = dot_nt(q_nope, v) + dot_nt(query_rope[i], keys[:, rows * KV_RANK :])
            s = jnp.where(col < live[i] - limit, s * scale, -jnp.inf)
            old = top[i]
            peak = jnp.maximum(old, jnp.max(s, axis=1, keepdims=True))
            shrink = jnp.exp(old - peak)
            w = jnp.exp(s - peak)
            top[i] = peak
            total[i] = total[i] * shrink + w
            acc[i] = acc[i] * wide(shrink) + dot_nn(w.astype(jnp.bfloat16), v)

    def take_half(source, half, last):
        limit = source * block + half * piece
        for i in range(rows):
            keys = recv[source, half]
            q_nope = query_v[:, i].reshape(queries_n, width)[:, :KV_RANK]
            v = keys[:, i * KV_RANK : (i + 1) * KV_RANK]
            s = dot_nt(q_nope, v) + dot_nt(query_rope[i], keys[:, rows * KV_RANK :])
            s = jnp.where(col[:, :piece] < live[i] - limit, s * scale, -jnp.inf)
            old = top[i]
            peak = jnp.maximum(old, jnp.max(s, axis=1, keepdims=True))
            shrink = jnp.exp(old - peak)
            w = jnp.exp(s - peak[:, :piece])
            mixed = acc[i] * wide(shrink) + dot_nn(w.astype(jnp.bfloat16), v)
            if last:
                mass = jnp.sum(total[i] * shrink, axis=1, keepdims=True)
                mass = mass + jnp.sum(w, axis=1, keepdims=True)
                mixed = (mixed * (1.0 / mass)).astype(out_ref.dtype)
                out_ref[:, i] = mixed.reshape(steps, heads, KV_RANK)
            else:
                top[i] = peak
                total[i] = total[i] * shrink
                total[i, :, :piece] += w
                acc[i] = mixed

    own_relay.wait_recv()
    take_in(me)
    for step in range(peers - 2):
        for arrival in arrivals[step]:
            arrival.wait_recv()
        relays[step].start()
        if step:
            relays[step - 1].wait_recv()
            take_in(sources[step - 1])
    relays[peers - 3].wait_recv()
    take_in(sources[-2])
    for arrival, relay in zip(arrivals[-1], relays[-2:]):
        arrival.wait_recv()
        relay.start()
    take_half(sources[-1], core, False)
    for relay in relays[-2:]:
        relay.wait_recv()
    take_half(sources[-1], mate, True)
    for copy in sends:
        copy.wait_send()
    for relay in relays + [own_relay]:
        relay.wait_send()


def direct(prompt_latent, row_cache, queries, new_latent, prompt_len, assign, row_ctx):
    peers = lax.axis_size("row")
    steps, rows, heads, width = queries.shape
    rope = width - KV_RANK
    local = prompt_latent.reshape(prompt_latent.shape[1:])
    cache_t = jnp.swapaxes(row_cache, 1, 2)
    piece = local.shape[1]
    lanes = rows * rope
    packed = rows * KV_RANK + lanes
    total_n = steps * heads
    bf16, f32 = jnp.bfloat16, jnp.float32
    hbm = pl.BlockSpec(memory_space=pl.ANY)
    smem = pl.BlockSpec(memory_space=pltpu.SMEM)
    return pl.pallas_call(
        functools.partial(fused, (NOPE_DIM + ROPE_DIM) ** (-0.5)),
        out_shape=pltpu.VMEM((steps, rows, heads, KV_RANK), bf16),
        in_specs=[hbm, hbm, hbm, hbm, smem, smem, smem],
        out_specs=pl.BlockSpec(memory_space=pltpu.VMEM),
        scratch_shapes=[
            pltpu.VMEM(local.shape, bf16),
            pltpu.VMEM(cache_t.shape, bf16),
            pltpu.VMEM(queries.shape, bf16),
            pltpu.VMEM(new_latent.shape, bf16),
            pltpu.VMEM((rows, lanes, width), bf16),
            pltpu.VMEM((rows, total_n, lanes), bf16),
            pltpu.VMEM((peers - 1, piece, packed), bf16),
            pltpu.VMEM((peers, 2, piece, packed), bf16),
            pltpu.VMEM((rows, total_n, KV_RANK), f32),
            pltpu.VMEM((rows, total_n, lanes), f32),
            pltpu.VMEM((rows, total_n, lanes), f32),
            pltpu.SemaphoreType.DMA((3,)),
            pltpu.SemaphoreType.DMA((4,)),
            pltpu.SemaphoreType.DMA((peers - 1, 2)),
            pltpu.SemaphoreType.DMA((peers, 2)),
            pltpu.SemaphoreType.DMA((peers + 1,)),
            pltpu.SemaphoreType.DMA((peers + 1,)),
            pltpu.SemaphoreType.REGULAR((peers,)),
        ],
        compiler_params=pltpu.CompilerParams(collective_id=0, has_side_effects=True),
    )(local, cache_t, queries, new_latent, prompt_len, assign, row_ctx)


def solution(mesh):
    one_group = mesh.shape["row"] == SPR and mesh.shape["tp"] == 2
    return jax.shard_map(
        direct if one_group else shards,
        mesh=mesh,
        in_specs=(
            P(("group", "row"), None, "tp", None),
            P(("group", "row"), None, None),
            P(None, ("group", "row"), "tp", None),
            P(None, ("group", "row"), None),
            P("group"),
            P("group"),
            P(("group", "row")),
        ),
        out_specs=P(None, ("group", "row"), "tp", None),
        check_vma=False,
    )
```

```python
import functools

import jax
import jax.numpy as jnp
from jax import lax
from jax.experimental import pallas as pl
from jax.experimental.pallas import tpu as pltpu
from jax.sharding import PartitionSpec as P

KV_RANK = 512
ROPE_DIM = 64
NOPE_DIM = 128
SPR = 8


def pick(array, index):
    return lax.map(lambda i: lax.dynamic_index_in_dim(array, i, 0, keepdims=False), index)


def shards(prompt_latent, row_cache, queries, new_latent, prompt_len, assign, row_ctx):
    row_count = lax.axis_size("row")
    pair_count = lax.axis_size("tp")
    row_place = lax.axis_index("row")
    rows_here = row_cache.shape[0]
    group_rows = prompt_latent.shape[1]
    piece_len = prompt_latent.shape[2]
    latent_width = prompt_latent.shape[3]
    full_len = piece_len * SPR * pair_count
    most_slots = min(rows_here, max(2, 2 * rows_here * SPR // row_count))
    home_group = row_place // SPR
    dest_prompt = assign.reshape(row_count, rows_here)
    in_group = dest_prompt // group_rows == home_group
    row_ids = jnp.arange(rows_here, dtype=jnp.int32)
    up_to = row_ids[:, None] <= row_ids[None, :]
    rank = jnp.sum((in_group[:, :, None] & up_to[None]).astype(jnp.int32), axis=1) - 1
    slot_ids = jnp.arange(most_slots, dtype=jnp.int32)
    picked = in_group[:, :, None] & (rank[:, :, None] == slot_ids[None, None, :])
    local_id = dest_prompt - home_group * group_rows
    source_index = jnp.sum(jnp.where(picked, local_id[:, :, None], 0), axis=1)
    filled = jnp.any(picked, axis=1).reshape(-1)
    owned = lax.dynamic_slice_in_dim(assign, row_place * rows_here, rows_here)
    owned_group = owned // group_rows
    same_before = (owned_group[:, None] == owned_group[None, :]) & (
        row_ids[None, :] < row_ids[:, None]
    )
    own_rank = jnp.sum(same_before.astype(jnp.int32), axis=1)
    block_ids = jnp.arange(SPR, dtype=jnp.int32)
    fetch_index = (
        (owned_group[:, None] * SPR + block_ids[None, :]) * most_slots + own_rank[:, None]
    ).reshape(-1)
    local = prompt_latent[0]
    rows_taken = pick(local, source_index.reshape(-1))
    rows_taken = jnp.where(filled[:, None, None], rows_taken, jnp.zeros_like(rows_taken))
    moved = lax.all_to_all(
        rows_taken.reshape((row_count, most_slots) + local.shape[1:]),
        "row",
        split_axis=0,
        concat_axis=0,
        tiled=True,
    )
    flat = moved.reshape(row_count * most_slots, piece_len, latent_width)
    mine = pick(flat, fetch_index).reshape(rows_here, SPR, 1, piece_len, latent_width)
    paired = lax.all_gather(mine, "tp", axis=2, tiled=True)
    latents = paired.reshape(rows_here, full_len, latent_width)
    live_len = pick(prompt_len, owned)
    scale_factor = (NOPE_DIM + ROPE_DIM) ** (-0.5)
    steps_count = queries.shape[0]
    cache_len = row_cache.shape[1]
    cache_scores = (
        jnp.einsum("srhc,rkc->rshk", queries, row_cache, preferred_element_type=jnp.float32)
        * scale_factor
    )
    cache_live = jnp.arange(cache_len, dtype=jnp.int32)[None, :] < row_ctx[:, None]
    cache_scores = jnp.where(cache_live[:, None, None, :], cache_scores, -jnp.inf)
    fresh_scores = (
        jnp.einsum("srhc,jrc->rshj", queries, new_latent, preferred_element_type=jnp.float32)
        * scale_factor
    )
    step_ids = jnp.arange(steps_count, dtype=jnp.int32)
    causal = step_ids[None, :] <= step_ids[:, None]
    fresh_scores = jnp.where(causal[None, :, None, :], fresh_scores, -jnp.inf)
    prompt_live = jnp.arange(full_len, dtype=jnp.int32)[None, :] < live_len[:, None]
    prompt_scores = (
        jnp.einsum("srhc,rkc->rshk", queries, latents, preferred_element_type=jnp.float32)
        * scale_factor
    )
    prompt_scores = jnp.where(prompt_live[:, None, None, :], prompt_scores, -jnp.inf)
    row_top = jnp.maximum(
        jnp.max(prompt_scores, axis=3, keepdims=True),
        jnp.maximum(
            jnp.max(cache_scores, axis=3, keepdims=True),
            jnp.max(fresh_scores, axis=3, keepdims=True),
        ),
    )
    prompt_exp = jnp.exp(prompt_scores - row_top)
    cache_exp = jnp.exp(cache_scores - row_top)
    fresh_exp = jnp.exp(fresh_scores - row_top)
    denominator = (
        jnp.sum(prompt_exp, axis=3, keepdims=True)
        + jnp.sum(cache_exp, axis=3, keepdims=True)
        + jnp.sum(fresh_exp, axis=3, keepdims=True)
    )
    prompt_probs = (prompt_exp / denominator).astype(jnp.bfloat16)
    cache_probs = (cache_exp / denominator).astype(jnp.bfloat16)
    fresh_probs = (fresh_exp / denominator).astype(jnp.bfloat16)
    cache_out = jnp.einsum(
        "rshk,rkc->srhc", cache_probs, row_cache[:, :, :KV_RANK], preferred_element_type=jnp.float32
    )
    fresh_out = jnp.einsum(
        "rshj,jrc->srhc",
        fresh_probs,
        new_latent[:, :, :KV_RANK],
        preferred_element_type=jnp.float32,
    )
    prompt_out = jnp.einsum(
        "rshk,rkc->srhc", prompt_probs, latents[:, :, :KV_RANK], preferred_element_type=jnp.float32
    )
    return (prompt_out + cache_out + fresh_out).astype(jnp.bfloat16)


MESH = pl.DeviceIdType.MESH


LEVELS = (1, 0, 0, 2)
SENDS = (
    ((2, 0), (2, 1), (1, 0), (1, 1), (0, 1), (3, 0), (3, 1)),
    ((2, 0), (2, 1), (1, 1), (0, 0), (0, 1), (3, 0), (3, 1)),
    ((1, 0), (0, 0), (0, 1), (1, 1), (2, 1), (3, 0), (3, 1)),
    ((1, 0), (1, 1), (2, 0), (2, 1), (0, 0), (0, 1), (3, 1)),
)
TAKES = (
    ((0, 1), (1, 0), (1, 1), (2, 0), (3, 0), (3, 1), (2, 1)),
    ((1, 1), (3, 0), (3, 1), (2, 0), (0, 0), (0, 1), (2, 1)),
    ((0, 0), (0, 1), (2, 1), (1, 0), (3, 0), (3, 1), (1, 1)),
    ((3, 1), (2, 0), (2, 1), (0, 0), (0, 1), (1, 0), (1, 1)),
)


def by_rank(rank, a, b, c, d):
    high, low = rank // 2, rank % 2
    return (1 - high) * ((1 - low) * a + low * b) + high * ((1 - low) * c + low * d)


def peers_of(me, table):
    rank, side = me // 2, me % 2
    found = []
    for step in zip(*table):
        other = by_rank(rank, *(entry[1] for entry in step))
        found.append(2 * by_rank(rank, *(entry[0] for entry in step)) + side + other - 2 * side * other)
    return found


def fused(
    scale,
    prompt_hbm,
    cache_hbm,
    query_hbm,
    fresh_hbm,
    plen_ref,
    assign_ref,
    ctx_ref,
    out_ref,
    prompt_v,
    cache_v,
    query_v,
    fresh_v,
    fresh_keys,
    query_rope,
    send,
    recv,
    acc,
    top,
    total,
    load_sem,
    prompt_sem,
    send_sem,
    recv_sem,
    relay_sem,
    relayed_sem,
    ready,
):
    me = lax.axis_index("row")
    core = lax.axis_index("tp")
    mate = 1 - core
    targets, sources = peers_of(me, SENDS), peers_of(me, TAKES)
    peers = len(targets) + 1
    rows = cache_v.shape[0]
    cache_len = cache_v.shape[2]
    steps, _, heads, width = query_v.shape
    rope = width - KV_RANK
    piece = prompt_v.shape[1]
    block = 2 * piece
    lanes = rows * rope
    queries_n = steps * heads

    loads = [
        pltpu.make_async_copy(source, target, load_sem.at[i])
        for i, (source, target) in enumerate(
            (
                (query_hbm, query_v),
                (cache_hbm, cache_v),
                (fresh_hbm, fresh_v),
            )
        )
    ]
    prompt_loads = [
        pltpu.make_async_copy(prompt_hbm.at[i], prompt_v.at[i], prompt_sem.at[i])
        for i in range(prompt_v.shape[0])
    ]
    for load in prompt_loads:
        load.start()

    barrier = pltpu.get_barrier_semaphore()

    def tell(semaphore, row):
        pl.semaphore_signal(semaphore, inc=1, device_id={"row": row}, device_id_type=MESH)

    pl.semaphore_signal(barrier, inc=1, device_id={"tp": mate}, device_id_type=MESH)
    level = by_rank(me // 2, *LEVELS)
    row_levels = [LEVELS[row // 2] for row in range(peers)]
    for row, its in enumerate(row_levels):

        @pl.when((row != me) & (its >= level))
        def _():
            tell(barrier, row)

    pl.semaphore_wait(barrier, by_rank(me // 2, *(sum(its <= LEVELS[r] for its in row_levels) for r in range(4))))
    for row, its in enumerate(row_levels):

        @pl.when(its < level)
        def _():
            tell(ready.at[me], row)

    for load in prompt_loads:
        load.wait()

    def pack(dest, target):
        tails = []
        for i in range(rows):
            taken = prompt_v[assign_ref[dest * rows + i]]
            target[:, i * KV_RANK : (i + 1) * KV_RANK] = taken[:, :KV_RANK]
            tails.append(taken[:, KV_RANK:])
        target[:, rows * KV_RANK :] = jnp.concatenate(tails, axis=1)

    early = piece * 3 // 4
    cuts = [pl.ds(0, early), pl.ds(early, piece - early)]
    whole = pl.ds(0, piece)

    def copy_to(step, target, source, cut):
        return pltpu.make_async_remote_copy(
            src_ref=send.at[step, cuts[cut]],
            dst_ref=recv.at[source, core, cuts[cut]],
            send_sem=send_sem.at[step, cut],
            recv_sem=recv_sem.at[source, cut],
            device_id={"row": target},
            device_id_type=MESH,
        )

    def relay_of(step, source, part):
        return pltpu.make_async_remote_copy(
            src_ref=recv.at[source, core, part],
            dst_ref=recv.at[source, core, part],
            send_sem=relay_sem.at[step],
            recv_sem=relayed_sem.at[step],
            device_id={"tp": mate},
            device_id_type=MESH,
        )

    sends = []
    for step, target in enumerate(targets):
        pack(target, send.at[step])

        @pl.when(by_rank(target // 2, *LEVELS) > level)
        def _():
            pl.semaphore_wait(ready.at[target], 1)

        for cut in range(2):
            copy = copy_to(step, target, me, cut)
            copy.start()
            sends.append(copy)
    for load in loads:
        load.start()
    arrivals = [[copy_to(step, source, source, cut) for cut in range(2)] for step, source in enumerate(sources)]
    relays = [relay_of(step, source, whole) for step, source in enumerate(sources[:-1])]
    relays += [relay_of(peers - 2 + cut, sources[-1], cuts[cut]) for cut in range(2)]
    own_relay = relay_of(peers, me, whole)
    pack(me, recv.at[me, core])
    own_relay.start()
    fresh_keys[...] = jnp.zeros_like(fresh_keys)
    query_rope[...] = jnp.zeros_like(query_rope)

    for load in loads:
        load.wait()
    nt = (((1,), (1,)), ((), ()))

    def dot_nt(a, b):
        return lax.dot_general(a, b, nt, preferred_element_type=jnp.float32)

    def dot_nn(a, b):
        return jnp.dot(a, b, preferred_element_type=jnp.float32)

    def wide(x):
        return jnp.concatenate([x] * (KV_RANK // lanes), axis=1)

    col = lax.broadcasted_iota(jnp.int32, (queries_n, lanes), 1)
    step_of = lax.broadcasted_iota(jnp.int32, (queries_n, lanes), 0) // heads
    live = [plen_ref[assign_ref[me * rows + i]] for i in range(rows)]
    for i in range(rows):
        q = query_v[:, i].reshape(queries_n, width)
        q_nope, q_rope = q[:, :KV_RANK], q[:, KV_RANK:]
        query_rope[i, :, i * rope : (i + 1) * rope] = q_rope
        fresh_keys[i, :steps, :] = fresh_v[:, i, :]
        ctx = ctx_ref[i]
        parts = []
        values = []
        for first in range(0, cache_len, lanes):
            keys = cache_v[i, :, first : first + lanes]
            s = dot_nn(q_nope, keys[:KV_RANK]) + dot_nn(q_rope, keys[KV_RANK:])
            parts.append(jnp.where(col + first < ctx, s * scale, -jnp.inf))
            values.append(keys[:KV_RANK])
        keys = fresh_keys[i]
        s = dot_nt(q_nope, keys[:, :KV_RANK]) + dot_nt(q_rope, keys[:, KV_RANK:])
        parts.append(jnp.where(col <= step_of, s * scale, -jnp.inf))
        peak = parts[0]
        for s in parts[1:]:
            peak = jnp.maximum(peak, s)
        peak = jnp.broadcast_to(jnp.max(peak, axis=1, keepdims=True), (queries_n, lanes))
        top[i] = peak
        weights = [jnp.exp(s - peak) for s in parts]
        total[i] = sum(weights[1:], weights[0])
        out = dot_nn(weights[-1].astype(jnp.bfloat16), keys[:, :KV_RANK])
        for w, v in zip(weights, values):
            out = out + dot_nt(w.astype(jnp.bfloat16), v)
        acc[i] = out

    def take_in(source):
        limit = source * block
        for i in range(rows):
            keys = recv[source].reshape(block, rows * KV_RANK + lanes)
            q_nope = query_v[:, i].reshape(queries_n, width)[:, :KV_RANK]
            v = keys[:, i * KV_RANK : (i + 1) * KV_RANK]
            s = dot_nt(q_nope, v) + dot_nt(query_rope[i], keys[:, rows * KV_RANK :])
            s = jnp.where(col < live[i] - limit, s * scale, -jnp.inf)
            old = top[i]
            peak = jnp.maximum(old, jnp.max(s, axis=1, keepdims=True))
            shrink = jnp.exp(old - peak)
            w = jnp.exp(s - peak)
            top[i] = peak
            total[i] = total[i] * shrink + w
            acc[i] = acc[i] * wide(shrink) + dot_nn(w.astype(jnp.bfloat16), v)

    def take_half(source, half, last):
        limit = source * block + half * piece
        for i in range(rows):
            keys = recv[source, half]
            q_nope = query_v[:, i].reshape(queries_n, width)[:, :KV_RANK]
            v = keys[:, i * KV_RANK : (i + 1) * KV_RANK]
            s = dot_nt(q_nope, v) + dot_nt(query_rope[i], keys[:, rows * KV_RANK :])
            s = jnp.where(col[:, :piece] < live[i] - limit, s * scale, -jnp.inf)
            old = top[i]
            peak = jnp.maximum(old, jnp.max(s, axis=1, keepdims=True))
            shrink = jnp.exp(old - peak)
            w = jnp.exp(s - peak[:, :piece])
            mixed = acc[i] * wide(shrink) + dot_nn(w.astype(jnp.bfloat16), v)
            if last:
                mass = jnp.sum(total[i] * shrink, axis=1, keepdims=True)
                mass = mass + jnp.sum(w, axis=1, keepdims=True)
                mixed = (mixed * (1.0 / mass)).astype(out_ref.dtype)
                out_ref[:, i] = mixed.reshape(steps, heads, KV_RANK)
            else:
                top[i] = peak
                total[i] = total[i] * shrink
                total[i, :, :piece] += w
                acc[i] = mixed

    own_relay.wait_recv()
    take_in(me)
    for step in range(peers - 2):
        for arrival in arrivals[step]:
            arrival.wait_recv()
        relays[step].start()
        if step:
            relays[step - 1].wait_recv()
            take_in(sources[step - 1])
    relays[peers - 3].wait_recv()
    take_in(sources[-2])
    for arrival, relay in zip(arrivals[-1], relays[-2:]):
        arrival.wait_recv()
        relay.start()
    take_half(sources[-1], core, False)
    for relay in relays[-2:]:
        relay.wait_recv()
    take_half(sources[-1], mate, True)
    for copy in sends:
        copy.wait_send()
    for relay in relays + [own_relay]:
        relay.wait_send()


def direct(prompt_latent, row_cache, queries, new_latent, prompt_len, assign, row_ctx):
    peers = lax.axis_size("row")
    steps, rows, heads, width = queries.shape
    rope = width - KV_RANK
    local = prompt_latent.reshape(prompt_latent.shape[1:])
    cache_t = jnp.swapaxes(row_cache, 1, 2)
    piece = local.shape[1]
    lanes = rows * rope
    packed = rows * KV_RANK + lanes
    total_n = steps * heads
    bf16, f32 = jnp.bfloat16, jnp.float32
    hbm = pl.BlockSpec(memory_space=pl.ANY)
    smem = pl.BlockSpec(memory_space=pltpu.SMEM)
    return pl.pallas_call(
        functools.partial(fused, (NOPE_DIM + ROPE_DIM) ** (-0.5)),
        out_shape=pltpu.VMEM((steps, rows, heads, KV_RANK), bf16),
        in_specs=[hbm, hbm, hbm, hbm, smem, smem, smem],
        out_specs=pl.BlockSpec(memory_space=pltpu.VMEM),
        scratch_shapes=[
            pltpu.VMEM(local.shape, bf16),
            pltpu.VMEM(cache_t.shape, bf16),
            pltpu.VMEM(queries.shape, bf16),
            pltpu.VMEM(new_latent.shape, bf16),
            pltpu.VMEM((rows, lanes, width), bf16),
            pltpu.VMEM((rows, total_n, lanes), bf16),
            pltpu.VMEM((peers - 1, piece, packed), bf16),
            pltpu.VMEM((peers, 2, piece, packed), bf16),
            pltpu.VMEM((rows, total_n, KV_RANK), f32),
            pltpu.VMEM((rows, total_n, lanes), f32),
            pltpu.VMEM((rows, total_n, lanes), f32),
            pltpu.SemaphoreType.DMA((3,)),
            pltpu.SemaphoreType.DMA((local.shape[0],)),
            pltpu.SemaphoreType.DMA((peers - 1, 2)),
            pltpu.SemaphoreType.DMA((peers, 2)),
            pltpu.SemaphoreType.DMA((peers + 1,)),
            pltpu.SemaphoreType.DMA((peers + 1,)),
            pltpu.SemaphoreType.REGULAR((peers,)),
        ],
        compiler_params=pltpu.CompilerParams(collective_id=0, has_side_effects=True),
    )(local, cache_t, queries, new_latent, prompt_len, assign, row_ctx)


def solution(mesh):
    one_group = mesh.shape["row"] == SPR and mesh.shape["tp"] == 2
    return jax.shard_map(
        direct if one_group else shards,
        mesh=mesh,
        in_specs=(
            P(("group", "row"), None, "tp", None),
            P(("group", "row"), None, None),
            P(None, ("group", "row"), "tp", None),
            P(None, ("group", "row"), None),
            P("group"),
            P("group"),
            P(("group", "row")),
        ),
        out_specs=P(None, ("group", "row"), "tp", None),
        check_vma=False,
    )
```

```python
import functools

import jax
import jax.numpy as jnp
from jax import lax
from jax.experimental import pallas as pl
from jax.experimental.pallas import tpu as pltpu
from jax.sharding import PartitionSpec as P

KV_RANK = 512
ROPE_DIM = 64
NOPE_DIM = 128
SPR = 8


def pick(array, index):
    return lax.map(lambda i: lax.dynamic_index_in_dim(array, i, 0, keepdims=False), index)


def shards(prompt_latent, row_cache, queries, new_latent, prompt_len, assign, row_ctx):
    row_count = lax.axis_size("row")
    pair_count = lax.axis_size("tp")
    row_place = lax.axis_index("row")
    rows_here = row_cache.shape[0]
    group_rows = prompt_latent.shape[1]
    piece_len = prompt_latent.shape[2]
    latent_width = prompt_latent.shape[3]
    full_len = piece_len * SPR * pair_count
    most_slots = min(rows_here, max(2, 2 * rows_here * SPR // row_count))
    home_group = row_place // SPR
    dest_prompt = assign.reshape(row_count, rows_here)
    in_group = dest_prompt // group_rows == home_group
    row_ids = jnp.arange(rows_here, dtype=jnp.int32)
    up_to = row_ids[:, None] <= row_ids[None, :]
    rank = jnp.sum((in_group[:, :, None] & up_to[None]).astype(jnp.int32), axis=1) - 1
    slot_ids = jnp.arange(most_slots, dtype=jnp.int32)
    picked = in_group[:, :, None] & (rank[:, :, None] == slot_ids[None, None, :])
    local_id = dest_prompt - home_group * group_rows
    source_index = jnp.sum(jnp.where(picked, local_id[:, :, None], 0), axis=1)
    filled = jnp.any(picked, axis=1).reshape(-1)
    owned = lax.dynamic_slice_in_dim(assign, row_place * rows_here, rows_here)
    owned_group = owned // group_rows
    same_before = (owned_group[:, None] == owned_group[None, :]) & (
        row_ids[None, :] < row_ids[:, None]
    )
    own_rank = jnp.sum(same_before.astype(jnp.int32), axis=1)
    block_ids = jnp.arange(SPR, dtype=jnp.int32)
    fetch_index = (
        (owned_group[:, None] * SPR + block_ids[None, :]) * most_slots + own_rank[:, None]
    ).reshape(-1)
    local = prompt_latent[0]
    rows_taken = pick(local, source_index.reshape(-1))
    rows_taken = jnp.where(filled[:, None, None], rows_taken, jnp.zeros_like(rows_taken))
    moved = lax.all_to_all(
        rows_taken.reshape((row_count, most_slots) + local.shape[1:]),
        "row",
        split_axis=0,
        concat_axis=0,
        tiled=True,
    )
    flat = moved.reshape(row_count * most_slots, piece_len, latent_width)
    mine = pick(flat, fetch_index).reshape(rows_here, SPR, 1, piece_len, latent_width)
    paired = lax.all_gather(mine, "tp", axis=2, tiled=True)
    latents = paired.reshape(rows_here, full_len, latent_width)
    live_len = pick(prompt_len, owned)
    scale_factor = (NOPE_DIM + ROPE_DIM) ** (-0.5)
    steps_count = queries.shape[0]
    cache_len = row_cache.shape[1]
    cache_scores = (
        jnp.einsum("srhc,rkc->rshk", queries, row_cache, preferred_element_type=jnp.float32)
        * scale_factor
    )
    cache_live = jnp.arange(cache_len, dtype=jnp.int32)[None, :] < row_ctx[:, None]
    cache_scores = jnp.where(cache_live[:, None, None, :], cache_scores, -jnp.inf)
    fresh_scores = (
        jnp.einsum("srhc,jrc->rshj", queries, new_latent, preferred_element_type=jnp.float32)
        * scale_factor
    )
    step_ids = jnp.arange(steps_count, dtype=jnp.int32)
    causal = step_ids[None, :] <= step_ids[:, None]
    fresh_scores = jnp.where(causal[None, :, None, :], fresh_scores, -jnp.inf)
    prompt_live = jnp.arange(full_len, dtype=jnp.int32)[None, :] < live_len[:, None]
    prompt_scores = (
        jnp.einsum("srhc,rkc->rshk", queries, latents, preferred_element_type=jnp.float32)
        * scale_factor
    )
    prompt_scores = jnp.where(prompt_live[:, None, None, :], prompt_scores, -jnp.inf)
    row_top = jnp.maximum(
        jnp.max(prompt_scores, axis=3, keepdims=True),
        jnp.maximum(
            jnp.max(cache_scores, axis=3, keepdims=True),
            jnp.max(fresh_scores, axis=3, keepdims=True),
        ),
    )
    prompt_exp = jnp.exp(prompt_scores - row_top)
    cache_exp = jnp.exp(cache_scores - row_top)
    fresh_exp = jnp.exp(fresh_scores - row_top)
    denominator = (
        jnp.sum(prompt_exp, axis=3, keepdims=True)
        + jnp.sum(cache_exp, axis=3, keepdims=True)
        + jnp.sum(fresh_exp, axis=3, keepdims=True)
    )
    prompt_probs = (prompt_exp / denominator).astype(jnp.bfloat16)
    cache_probs = (cache_exp / denominator).astype(jnp.bfloat16)
    fresh_probs = (fresh_exp / denominator).astype(jnp.bfloat16)
    cache_out = jnp.einsum(
        "rshk,rkc->srhc", cache_probs, row_cache[:, :, :KV_RANK], preferred_element_type=jnp.float32
    )
    fresh_out = jnp.einsum(
        "rshj,jrc->srhc",
        fresh_probs,
        new_latent[:, :, :KV_RANK],
        preferred_element_type=jnp.float32,
    )
    prompt_out = jnp.einsum(
        "rshk,rkc->srhc", prompt_probs, latents[:, :, :KV_RANK], preferred_element_type=jnp.float32
    )
    return (prompt_out + cache_out + fresh_out).astype(jnp.bfloat16)


MESH = pl.DeviceIdType.MESH


LEVELS = (1, 0, 0, 2)
SENDS = (
    (4, 5, 2, 3, 1, 6, 7),
    (5, 4, 3, 2, 0, 7, 6),
    (4, 5, 3, 0, 1, 6, 7),
    (5, 4, 2, 1, 0, 7, 6),
    (2, 0, 1, 3, 5, 6, 7),
    (2, 0, 1, 3, 4, 7, 6),
    (2, 3, 4, 5, 0, 1, 7),
    (3, 2, 5, 4, 1, 0, 6),
)
TAKES = (
    (1, 2, 3, 4, 5, 6, 7),
    (0, 3, 2, 7, 6, 5, 4),
    (3, 6, 7, 4, 5, 0, 1),
    (2, 7, 6, 1, 0, 5, 4),
    (0, 1, 5, 2, 6, 7, 3),
    (1, 0, 4, 3, 7, 6, 2),
    (7, 4, 5, 0, 1, 2, 3),
    (6, 5, 4, 1, 0, 3, 2),
)
TOGETHER = (1, 3)


def by_rank(rank, a, b, c, d):
    high, low = rank // 2, rank % 2
    return (1 - high) * ((1 - low) * a + low * b) + high * ((1 - low) * c + low * d)


def peers_of(me, table):
    rank, side = me // 2, me % 2
    return [(1 - side) * by_rank(rank, *step[::2]) + side * by_rank(rank, *step[1::2]) for step in zip(*table)]


def fused(
    scale,
    prompt_hbm,
    cache_hbm,
    query_hbm,
    fresh_hbm,
    plen_ref,
    assign_ref,
    ctx_ref,
    out_ref,
    prompt_v,
    cache_v,
    query_v,
    fresh_v,
    fresh_keys,
    query_rope,
    send,
    recv,
    acc,
    top,
    total,
    load_sem,
    prompt_sem,
    send_sem,
    recv_sem,
    relay_sem,
    relayed_sem,
    ready,
):
    me = lax.axis_index("row")
    core = lax.axis_index("tp")
    mate = 1 - core
    targets, sources = peers_of(me, SENDS), peers_of(me, TAKES)
    peers = len(targets) + 1
    rows = cache_v.shape[0]
    cache_len = cache_v.shape[2]
    steps, _, heads, width = query_v.shape
    rope = width - KV_RANK
    piece = prompt_v.shape[1]
    block = 2 * piece
    lanes = rows * rope
    queries_n = steps * heads

    loads = [
        pltpu.make_async_copy(source, target, load_sem.at[i])
        for i, (source, target) in enumerate(
            (
                (query_hbm, query_v),
                (cache_hbm, cache_v),
                (fresh_hbm, fresh_v),
            )
        )
    ]
    groups = prompt_v.shape[0] // 4
    prompt_loads = [
        pltpu.make_async_copy(
            prompt_hbm.at[pl.ds(i * groups, groups)],
            prompt_v.at[pl.ds(i * groups, groups)],
            prompt_sem.at[i],
        )
        for i in range(4)
    ]
    for load in prompt_loads:
        load.start()

    barrier = pltpu.get_barrier_semaphore()

    def tell(semaphore, row):
        pl.semaphore_signal(semaphore, inc=1, device_id={"row": row}, device_id_type=MESH)

    pl.semaphore_signal(barrier, inc=1, device_id={"tp": mate}, device_id_type=MESH)
    level = by_rank(me // 2, *LEVELS)
    row_levels = [LEVELS[row // 2] for row in range(peers)]
    for row, its in enumerate(row_levels):

        @pl.when((row != me) & (its >= level))
        def _():
            tell(barrier, row)

    pl.semaphore_wait(barrier, by_rank(me // 2, *(sum(its <= LEVELS[r] for its in row_levels) for r in range(4))))
    for row, its in enumerate(row_levels):

        @pl.when(its < level)
        def _():
            tell(ready.at[me], row)

    for load in prompt_loads:
        load.wait()

    def pack(dest, target):
        tails = []
        for i in range(rows):
            taken = prompt_v[assign_ref[dest * rows + i]]
            target[:, i * KV_RANK : (i + 1) * KV_RANK] = taken[:, :KV_RANK]
            tails.append(taken[:, KV_RANK:])
        target[:, rows * KV_RANK :] = jnp.concatenate(tails, axis=1)

    early = piece * 3 // 4
    cuts = [pl.ds(0, early), pl.ds(early, piece - early)]
    whole = pl.ds(0, piece)

    def copy_to(step, target, source, cut):
        return pltpu.make_async_remote_copy(
            src_ref=send.at[step, cuts[cut]],
            dst_ref=recv.at[source, core, cuts[cut]],
            send_sem=send_sem.at[step, cut],
            recv_sem=recv_sem.at[source, cut],
            device_id={"row": target},
            device_id_type=MESH,
        )

    def relay_of(step, source, part):
        return pltpu.make_async_remote_copy(
            src_ref=recv.at[source, core, part],
            dst_ref=recv.at[source, core, part],
            send_sem=relay_sem.at[step],
            recv_sem=relayed_sem.at[step],
            device_id={"tp": mate},
            device_id_type=MESH,
        )

    sends = []
    for step, target in enumerate(targets):
        pack(target, send.at[step])

        @pl.when(by_rank(target // 2, *LEVELS) > level)
        def _():
            pl.semaphore_wait(ready.at[target], 1)

        for cut in range(2):
            copy = copy_to(step, target, me, cut)
            copy.start()
            sends.append(copy)
    for load in loads:
        load.start()
    arrivals = [[copy_to(step, source, source, cut) for cut in range(2)] for step, source in enumerate(sources)]
    relays = [relay_of(step, source, whole) for step, source in enumerate(sources[:-1])]
    relays += [relay_of(peers - 2 + cut, sources[-1], cuts[cut]) for cut in range(2)]
    own_relay = relay_of(peers, me, whole)
    pack(me, recv.at[me, core])
    own_relay.start()
    fresh_keys[...] = jnp.zeros_like(fresh_keys)
    query_rope[...] = jnp.zeros_like(query_rope)

    for load in loads:
        load.wait()
    nt = (((1,), (1,)), ((), ()))

    def dot_nt(a, b):
        return lax.dot_general(a, b, nt, preferred_element_type=jnp.float32)

    def dot_nn(a, b):
        return jnp.dot(a, b, preferred_element_type=jnp.float32)

    def wide(x):
        return jnp.concatenate([x] * (KV_RANK // lanes), axis=1)

    col = lax.broadcasted_iota(jnp.int32, (queries_n, lanes), 1)
    step_of = lax.broadcasted_iota(jnp.int32, (queries_n, lanes), 0) // heads
    live = [plen_ref[assign_ref[me * rows + i]] for i in range(rows)]
    for i in range(rows):
        q = query_v[:, i].reshape(queries_n, width)
        q_nope, q_rope = q[:, :KV_RANK], q[:, KV_RANK:]
        query_rope[i, :, i * rope : (i + 1) * rope] = q_rope
        fresh_keys[i, :steps, :] = fresh_v[:, i, :]
        ctx = ctx_ref[i]
        parts = []
        values = []
        for first in range(0, cache_len, lanes):
            keys = cache_v[i, :, first : first + lanes]
            s = dot_nn(q_nope, keys[:KV_RANK]) + dot_nn(q_rope, keys[KV_RANK:])
            parts.append(jnp.where(col + first < ctx, s * scale, -jnp.inf))
            values.append(keys[:KV_RANK])
        keys = fresh_keys[i]
        s = dot_nt(q_nope, keys[:, :KV_RANK]) + dot_nt(q_rope, keys[:, KV_RANK:])
        parts.append(jnp.where(col <= step_of, s * scale, -jnp.inf))
        peak = parts[0]
        for s in parts[1:]:
            peak = jnp.maximum(peak, s)
        peak = jnp.broadcast_to(jnp.max(peak, axis=1, keepdims=True), (queries_n, lanes))
        top[i] = peak
        weights = [jnp.exp(s - peak) for s in parts]
        total[i] = sum(weights[1:], weights[0])
        out = dot_nn(weights[-1].astype(jnp.bfloat16), keys[:, :KV_RANK])
        for w, v in zip(weights, values):
            out = out + dot_nt(w.astype(jnp.bfloat16), v)
        acc[i] = out

    def take_in(source):
        limit = source * block
        for i in range(rows):
            keys = recv[source].reshape(block, rows * KV_RANK + lanes)
            q_nope = query_v[:, i].reshape(queries_n, width)[:, :KV_RANK]
            v = keys[:, i * KV_RANK : (i + 1) * KV_RANK]
            s = dot_nt(q_nope, v) + dot_nt(query_rope[i], keys[:, rows * KV_RANK :])
            s = jnp.where(col < live[i] - limit, s * scale, -jnp.inf)
            old = top[i]
            peak = jnp.maximum(old, jnp.max(s, axis=1, keepdims=True))
            shrink = jnp.exp(old - peak)
            w = jnp.exp(s - peak)
            top[i] = peak
            total[i] = total[i] * shrink + w
            acc[i] = acc[i] * wide(shrink) + dot_nn(w.astype(jnp.bfloat16), v)

    def take_half(source, half, last):
        limit = source * block + half * piece
        for i in range(rows):
            keys = recv[source, half]
            q_nope = query_v[:, i].reshape(queries_n, width)[:, :KV_RANK]
            v = keys[:, i * KV_RANK : (i + 1) * KV_RANK]
            s = dot_nt(q_nope, v) + dot_nt(query_rope[i], keys[:, rows * KV_RANK :])
            s = jnp.where(col[:, :piece] < live[i] - limit, s * scale, -jnp.inf)
            old = top[i]
            peak = jnp.maximum(old, jnp.max(s, axis=1, keepdims=True))
            shrink = jnp.exp(old - peak)
            w = jnp.exp(s - peak[:, :piece])
            mixed = acc[i] * wide(shrink) + dot_nn(w.astype(jnp.bfloat16), v)
            if last:
                mass = jnp.sum(total[i] * shrink, axis=1, keepdims=True)
                mass = mass + jnp.sum(w, axis=1, keepdims=True)
                mixed = (mixed * (1.0 / mass)).astype(out_ref.dtype)
                out_ref[:, i] = mixed.reshape(steps, heads, KV_RANK)
            else:
                top[i] = peak
                total[i] = total[i] * shrink
                total[i, :, :piece] += w
                acc[i] = mixed

    own_relay.wait_recv()
    take_in(me)
    for step in range(peers - 2):
        for arrival in arrivals[step]:
            arrival.wait_recv()
        relays[step].start()
        if step:
            relays[step - 1].wait_recv()
            take_in(sources[step - 1])
    def hand_over_last():
        for arrival, relay in zip(arrivals[-1], relays[-2:]):
            arrival.wait_recv()
            relay.start()

    together = functools.reduce(jnp.logical_or, [me == row for row in TOGETHER])
    pl.when(together)(hand_over_last)
    relays[peers - 3].wait_recv()
    take_in(sources[-2])
    pl.when(jnp.logical_not(together))(hand_over_last)
    take_half(sources[-1], core, False)
    for relay in relays[-2:]:
        relay.wait_recv()
    take_half(sources[-1], mate, True)
    for copy in sends:
        copy.wait_send()
    for relay in relays + [own_relay]:
        relay.wait_send()


def direct(prompt_latent, row_cache, queries, new_latent, prompt_len, assign, row_ctx):
    peers = lax.axis_size("row")
    steps, rows, heads, width = queries.shape
    rope = width - KV_RANK
    local = prompt_latent.reshape(prompt_latent.shape[1:])
    cache_t = jnp.swapaxes(row_cache, 1, 2)
    piece = local.shape[1]
    lanes = rows * rope
    packed = rows * KV_RANK + lanes
    total_n = steps * heads
    bf16, f32 = jnp.bfloat16, jnp.float32
    hbm = pl.BlockSpec(memory_space=pl.ANY)
    smem = pl.BlockSpec(memory_space=pltpu.SMEM)
    return pl.pallas_call(
        functools.partial(fused, (NOPE_DIM + ROPE_DIM) ** (-0.5)),
        out_shape=pltpu.VMEM((steps, rows, heads, KV_RANK), bf16),
        in_specs=[hbm, hbm, hbm, hbm, smem, smem, smem],
        out_specs=pl.BlockSpec(memory_space=pltpu.VMEM),
        scratch_shapes=[
            pltpu.VMEM(local.shape, bf16),
            pltpu.VMEM(cache_t.shape, bf16),
            pltpu.VMEM(queries.shape, bf16),
            pltpu.VMEM(new_latent.shape, bf16),
            pltpu.VMEM((rows, lanes, width), bf16),
            pltpu.VMEM((rows, total_n, lanes), bf16),
            pltpu.VMEM((peers - 1, piece, packed), bf16),
            pltpu.VMEM((peers, 2, piece, packed), bf16),
            pltpu.VMEM((rows, total_n, KV_RANK), f32),
            pltpu.VMEM((rows, total_n, lanes), f32),
            pltpu.VMEM((rows, total_n, lanes), f32),
            pltpu.SemaphoreType.DMA((3,)),
            pltpu.SemaphoreType.DMA((4,)),
            pltpu.SemaphoreType.DMA((peers - 1, 2)),
            pltpu.SemaphoreType.DMA((peers, 2)),
            pltpu.SemaphoreType.DMA((peers + 1,)),
            pltpu.SemaphoreType.DMA((peers + 1,)),
            pltpu.SemaphoreType.REGULAR((peers,)),
        ],
        compiler_params=pltpu.CompilerParams(collective_id=0, has_side_effects=True),
    )(local, cache_t, queries, new_latent, prompt_len, assign, row_ctx)


def solution(mesh):
    one_group = mesh.shape["row"] == SPR and mesh.shape["tp"] == 2
    return jax.shard_map(
        direct if one_group else shards,
        mesh=mesh,
        in_specs=(
            P(("group", "row"), None, "tp", None),
            P(("group", "row"), None, None),
            P(None, ("group", "row"), "tp", None),
            P(None, ("group", "row"), None),
            P("group"),
            P("group"),
            P(("group", "row")),
        ),
        out_specs=P(None, ("group", "row"), "tp", None),
        check_vma=False,
    )
```

```python
import functools

import jax
import jax.numpy as jnp
from jax import lax
from jax.experimental import pallas as pl
from jax.experimental.pallas import tpu as pltpu
from jax.sharding import PartitionSpec as P

KV_RANK = 512
ROPE_DIM = 64
NOPE_DIM = 128
SPR = 8


def pick(array, index):
    return lax.map(lambda i: lax.dynamic_index_in_dim(array, i, 0, keepdims=False), index)


def shards(prompt_latent, row_cache, queries, new_latent, prompt_len, assign, row_ctx):
    row_count = lax.axis_size("row")
    pair_count = lax.axis_size("tp")
    row_place = lax.axis_index("row")
    rows_here = row_cache.shape[0]
    group_rows = prompt_latent.shape[1]
    piece_len = prompt_latent.shape[2]
    latent_width = prompt_latent.shape[3]
    full_len = piece_len * SPR * pair_count
    most_slots = min(rows_here, max(2, 2 * rows_here * SPR // row_count))
    home_group = row_place // SPR
    dest_prompt = assign.reshape(row_count, rows_here)
    in_group = dest_prompt // group_rows == home_group
    row_ids = jnp.arange(rows_here, dtype=jnp.int32)
    up_to = row_ids[:, None] <= row_ids[None, :]
    rank = jnp.sum((in_group[:, :, None] & up_to[None]).astype(jnp.int32), axis=1) - 1
    slot_ids = jnp.arange(most_slots, dtype=jnp.int32)
    picked = in_group[:, :, None] & (rank[:, :, None] == slot_ids[None, None, :])
    local_id = dest_prompt - home_group * group_rows
    source_index = jnp.sum(jnp.where(picked, local_id[:, :, None], 0), axis=1)
    filled = jnp.any(picked, axis=1).reshape(-1)
    owned = lax.dynamic_slice_in_dim(assign, row_place * rows_here, rows_here)
    owned_group = owned // group_rows
    same_before = (owned_group[:, None] == owned_group[None, :]) & (
        row_ids[None, :] < row_ids[:, None]
    )
    own_rank = jnp.sum(same_before.astype(jnp.int32), axis=1)
    block_ids = jnp.arange(SPR, dtype=jnp.int32)
    fetch_index = (
        (owned_group[:, None] * SPR + block_ids[None, :]) * most_slots + own_rank[:, None]
    ).reshape(-1)
    local = prompt_latent[0]
    rows_taken = pick(local, source_index.reshape(-1))
    rows_taken = jnp.where(filled[:, None, None], rows_taken, jnp.zeros_like(rows_taken))
    moved = lax.all_to_all(
        rows_taken.reshape((row_count, most_slots) + local.shape[1:]),
        "row",
        split_axis=0,
        concat_axis=0,
        tiled=True,
    )
    flat = moved.reshape(row_count * most_slots, piece_len, latent_width)
    mine = pick(flat, fetch_index).reshape(rows_here, SPR, 1, piece_len, latent_width)
    paired = lax.all_gather(mine, "tp", axis=2, tiled=True)
    latents = paired.reshape(rows_here, full_len, latent_width)
    live_len = pick(prompt_len, owned)
    scale_factor = (NOPE_DIM + ROPE_DIM) ** (-0.5)
    steps_count = queries.shape[0]
    cache_len = row_cache.shape[1]
    cache_scores = (
        jnp.einsum("srhc,rkc->rshk", queries, row_cache, preferred_element_type=jnp.float32)
        * scale_factor
    )
    cache_live = jnp.arange(cache_len, dtype=jnp.int32)[None, :] < row_ctx[:, None]
    cache_scores = jnp.where(cache_live[:, None, None, :], cache_scores, -jnp.inf)
    fresh_scores = (
        jnp.einsum("srhc,jrc->rshj", queries, new_latent, preferred_element_type=jnp.float32)
        * scale_factor
    )
    step_ids = jnp.arange(steps_count, dtype=jnp.int32)
    causal = step_ids[None, :] <= step_ids[:, None]
    fresh_scores = jnp.where(causal[None, :, None, :], fresh_scores, -jnp.inf)
    prompt_live = jnp.arange(full_len, dtype=jnp.int32)[None, :] < live_len[:, None]
    prompt_scores = (
        jnp.einsum("srhc,rkc->rshk", queries, latents, preferred_element_type=jnp.float32)
        * scale_factor
    )
    prompt_scores = jnp.where(prompt_live[:, None, None, :], prompt_scores, -jnp.inf)
    row_top = jnp.maximum(
        jnp.max(prompt_scores, axis=3, keepdims=True),
        jnp.maximum(
            jnp.max(cache_scores, axis=3, keepdims=True),
            jnp.max(fresh_scores, axis=3, keepdims=True),
        ),
    )
    prompt_exp = jnp.exp(prompt_scores - row_top)
    cache_exp = jnp.exp(cache_scores - row_top)
    fresh_exp = jnp.exp(fresh_scores - row_top)
    denominator = (
        jnp.sum(prompt_exp, axis=3, keepdims=True)
        + jnp.sum(cache_exp, axis=3, keepdims=True)
        + jnp.sum(fresh_exp, axis=3, keepdims=True)
    )
    prompt_probs = (prompt_exp / denominator).astype(jnp.bfloat16)
    cache_probs = (cache_exp / denominator).astype(jnp.bfloat16)
    fresh_probs = (fresh_exp / denominator).astype(jnp.bfloat16)
    cache_out = jnp.einsum(
        "rshk,rkc->srhc", cache_probs, row_cache[:, :, :KV_RANK], preferred_element_type=jnp.float32
    )
    fresh_out = jnp.einsum(
        "rshj,jrc->srhc",
        fresh_probs,
        new_latent[:, :, :KV_RANK],
        preferred_element_type=jnp.float32,
    )
    prompt_out = jnp.einsum(
        "rshk,rkc->srhc", prompt_probs, latents[:, :, :KV_RANK], preferred_element_type=jnp.float32
    )
    return (prompt_out + cache_out + fresh_out).astype(jnp.bfloat16)


MESH = pl.DeviceIdType.MESH


def flip(index, bits):
    out = index
    place = 1
    while place <= bits:
        if bits & place:
            out = out + place * (1 - 2 * ((index // place) % 2))
        place *= 2
    return out


def fused(
    order,
    scale,
    prompt_hbm,
    cache_hbm,
    query_hbm,
    fresh_hbm,
    plen_ref,
    assign_ref,
    ctx_ref,
    out_ref,
    prompt_v,
    cache_v,
    query_v,
    fresh_v,
    fresh_keys,
    query_rope,
    send,
    recv,
    acc,
    top,
    total,
    load_sem,
    prompt_sem,
    send_sem,
    recv_sem,
    relay_sem,
    relayed_sem,
):
    me = lax.axis_index("row")
    core = lax.axis_index("tp")
    mate = 1 - core
    peers = len(order) + 1
    rows = cache_v.shape[0]
    cache_len = cache_v.shape[2]
    steps, _, heads, width = query_v.shape
    rope = width - KV_RANK
    piece = prompt_v.shape[1]
    block = 2 * piece
    lanes = rows * rope
    queries_n = steps * heads

    loads = [
        pltpu.make_async_copy(source, target, load_sem.at[i])
        for i, (source, target) in enumerate(
            (
                (query_hbm, query_v),
                (cache_hbm, cache_v),
                (fresh_hbm, fresh_v),
            )
        )
    ]
    groups = prompt_v.shape[0] // 4
    prompt_loads = [
        pltpu.make_async_copy(
            prompt_hbm.at[pl.ds(i * groups, groups)],
            prompt_v.at[pl.ds(i * groups, groups)],
            prompt_sem.at[i],
        )
        for i in range(4)
    ]
    for load in prompt_loads:
        load.start()

    barrier = pltpu.get_barrier_semaphore()
    for bits in order:
        pl.semaphore_signal(barrier, inc=1, device_id={"row": flip(me, bits)}, device_id_type=MESH)
    pl.semaphore_signal(barrier, inc=1, device_id={"tp": mate}, device_id_type=MESH)

    fresh_keys[...] = jnp.zeros_like(fresh_keys)
    query_rope[...] = jnp.zeros_like(query_rope)

    for load in prompt_loads:
        load.wait()

    def pack(dest, target):
        tails = []
        for i in range(rows):
            taken = prompt_v[assign_ref[dest * rows + i]]
            target[:, i * KV_RANK : (i + 1) * KV_RANK] = taken[:, :KV_RANK]
            tails.append(taken[:, KV_RANK:])
        target[:, rows * KV_RANK :] = jnp.concatenate(tails, axis=1)

    for bits in order:
        pack(flip(me, bits), send.at[bits])
    pack(me, recv.at[0, core])

    pl.semaphore_wait(barrier, peers)

    final = order[-1]
    early = piece * 3 // 4
    cuts = [(bits, bits, 0, piece) for bits in order[:-1]]
    cuts += [(final, final, 0, early), (final, peers, early, piece - early)]
    sends = []
    for bits, at, first, count in cuts:
        part = pl.ds(first, count)
        copy = pltpu.make_async_remote_copy(
            src_ref=send.at[bits, part],
            dst_ref=recv.at[bits, core, part],
            send_sem=send_sem.at[at],
            recv_sem=recv_sem.at[at],
            device_id={"row": flip(me, bits)},
            device_id_type=MESH,
        )
        copy.start()
        sends.append(copy)
    for load in loads:
        load.start()
    relays = {}
    for bits, at, first, count in [(0, 0, 0, piece)] + cuts:
        part = pl.ds(first, count)
        relays[at] = pltpu.make_async_remote_copy(
            src_ref=recv.at[bits, core, part],
            dst_ref=recv.at[bits, core, part],
            send_sem=relay_sem.at[at],
            recv_sem=relayed_sem.at[at],
            device_id={"tp": mate},
            device_id_type=MESH,
        )
    relays[0].start()

    for load in loads:
        load.wait()
    nt = (((1,), (1,)), ((), ()))

    def dot_nt(a, b):
        return lax.dot_general(a, b, nt, preferred_element_type=jnp.float32)

    def dot_nn(a, b):
        return jnp.dot(a, b, preferred_element_type=jnp.float32)

    def wide(x):
        return jnp.concatenate([x] * (KV_RANK // lanes), axis=1)

    col = lax.broadcasted_iota(jnp.int32, (queries_n, lanes), 1)
    step_of = lax.broadcasted_iota(jnp.int32, (queries_n, lanes), 0) // heads
    live = [plen_ref[assign_ref[me * rows + i]] for i in range(rows)]
    for i in range(rows):
        q = query_v[:, i].reshape(queries_n, width)
        q_nope, q_rope = q[:, :KV_RANK], q[:, KV_RANK:]
        query_rope[i, :, i * rope : (i + 1) * rope] = q_rope
        fresh_keys[i, :steps, :] = fresh_v[:, i, :]
        ctx = ctx_ref[i]
        parts = []
        values = []
        for first in range(0, cache_len, lanes):
            keys = cache_v[i, :, first : first + lanes]
            s = dot_nn(q_nope, keys[:KV_RANK]) + dot_nn(q_rope, keys[KV_RANK:])
            parts.append(jnp.where(col + first < ctx, s * scale, -jnp.inf))
            values.append(keys[:KV_RANK])
        keys = fresh_keys[i]
        s = dot_nt(q_nope, keys[:, :KV_RANK]) + dot_nt(q_rope, keys[:, KV_RANK:])
        parts.append(jnp.where(col <= step_of, s * scale, -jnp.inf))
        peak = parts[0]
        for s in parts[1:]:
            peak = jnp.maximum(peak, s)
        peak = jnp.broadcast_to(jnp.max(peak, axis=1, keepdims=True), (queries_n, lanes))
        top[i] = peak
        weights = [jnp.exp(s - peak) for s in parts]
        total[i] = sum(weights[1:], weights[0])
        out = dot_nn(weights[-1].astype(jnp.bfloat16), keys[:, :KV_RANK])
        for w, v in zip(weights, values):
            out = out + dot_nt(w.astype(jnp.bfloat16), v)
        acc[i] = out

    def take_in(bits):
        limit = flip(me, bits) * block
        for i in range(rows):
            keys = recv[bits].reshape(block, rows * KV_RANK + lanes)
            q_nope = query_v[:, i].reshape(queries_n, width)[:, :KV_RANK]
            v = keys[:, i * KV_RANK : (i + 1) * KV_RANK]
            s = dot_nt(q_nope, v) + dot_nt(query_rope[i], keys[:, rows * KV_RANK :])
            s = jnp.where(col < live[i] - limit, s * scale, -jnp.inf)
            old = top[i]
            peak = jnp.maximum(old, jnp.max(s, axis=1, keepdims=True))
            shrink = jnp.exp(old - peak)
            w = jnp.exp(s - peak)
            top[i] = peak
            total[i] = total[i] * shrink + w
            acc[i] = acc[i] * wide(shrink) + dot_nn(w.astype(jnp.bfloat16), v)

    def take_half(bits, half, last):
        limit = flip(me, bits) * block + half * piece
        for i in range(rows):
            keys = recv[bits, half]
            q_nope = query_v[:, i].reshape(queries_n, width)[:, :KV_RANK]
            v = keys[:, i * KV_RANK : (i + 1) * KV_RANK]
            s = dot_nt(q_nope, v) + dot_nt(query_rope[i], keys[:, rows * KV_RANK :])
            s = jnp.where(col[:, :piece] < live[i] - limit, s * scale, -jnp.inf)
            old = top[i]
            peak = jnp.maximum(old, jnp.max(s, axis=1, keepdims=True))
            shrink = jnp.exp(old - peak)
            w = jnp.exp(s - peak[:, :piece])
            mixed = acc[i] * wide(shrink) + dot_nn(w.astype(jnp.bfloat16), v)
            if last:
                mass = jnp.sum(total[i] * shrink, axis=1, keepdims=True)
                mass = mass + jnp.sum(w, axis=1, keepdims=True)
                mixed = (mixed * (1.0 / mass)).astype(out_ref.dtype)
                out_ref[:, i] = mixed.reshape(steps, heads, KV_RANK)
            else:
                top[i] = peak
                total[i] = total[i] * shrink
                total[i, :, :piece] += w
                acc[i] = mixed

    relays[0].wait_recv()
    take_in(0)
    before = None
    for bits, copy in zip(order[:-1], sends):
        copy.wait_recv()
        relays[bits].start()
        if before is not None:
            relays[before].wait_recv()
            take_in(before)
        before = bits
    relays[before].wait_recv()
    take_in(before)
    for at, copy in zip((final, peers), sends[-2:]):
        copy.wait_recv()
        relays[at].start()
    take_half(final, core, False)
    for at in (final, peers):
        relays[at].wait_recv()
    take_half(final, mate, True)
    for copy in sends:
        copy.wait_send()
    for relay in relays.values():
        relay.wait_send()


def direct(prompt_latent, row_cache, queries, new_latent, prompt_len, assign, row_ctx):
    peers = lax.axis_size("row")
    order = (1, 2, 3) + tuple(range(4, peers))
    steps, rows, heads, width = queries.shape
    rope = width - KV_RANK
    local = prompt_latent.reshape(prompt_latent.shape[1:])
    cache_t = jnp.swapaxes(row_cache, 1, 2)
    piece = local.shape[1]
    lanes = rows * rope
    packed = rows * KV_RANK + lanes
    total_n = steps * heads
    bf16, f32 = jnp.bfloat16, jnp.float32
    hbm = pl.BlockSpec(memory_space=pl.ANY)
    smem = pl.BlockSpec(memory_space=pltpu.SMEM)
    return pl.pallas_call(
        functools.partial(fused, order, (NOPE_DIM + ROPE_DIM) ** (-0.5)),
        out_shape=pltpu.VMEM((steps, rows, heads, KV_RANK), bf16),
        in_specs=[hbm, hbm, hbm, hbm, smem, smem, smem],
        out_specs=pl.BlockSpec(memory_space=pltpu.VMEM),
        scratch_shapes=[
            pltpu.VMEM(local.shape, bf16),
            pltpu.VMEM(cache_t.shape, bf16),
            pltpu.VMEM(queries.shape, bf16),
            pltpu.VMEM(new_latent.shape, bf16),
            pltpu.VMEM((rows, lanes, width), bf16),
            pltpu.VMEM((rows, total_n, lanes), bf16),
            pltpu.VMEM((peers, piece, packed), bf16),
            pltpu.VMEM((peers, 2, piece, packed), bf16),
            pltpu.VMEM((rows, total_n, KV_RANK), f32),
            pltpu.VMEM((rows, total_n, lanes), f32),
            pltpu.VMEM((rows, total_n, lanes), f32),
            pltpu.SemaphoreType.DMA((3,)),
            pltpu.SemaphoreType.DMA((4,)),
            pltpu.SemaphoreType.DMA((peers + 1,)),
            pltpu.SemaphoreType.DMA((peers + 1,)),
            pltpu.SemaphoreType.DMA((peers + 1,)),
            pltpu.SemaphoreType.DMA((peers + 1,)),
        ],
        compiler_params=pltpu.CompilerParams(collective_id=0, has_side_effects=True),
    )(local, cache_t, queries, new_latent, prompt_len, assign, row_ctx)


def solution(mesh):
    one_group = mesh.shape["row"] == SPR and mesh.shape["tp"] == 2
    return jax.shard_map(
        direct if one_group else shards,
        mesh=mesh,
        in_specs=(
            P(("group", "row"), None, "tp", None),
            P(("group", "row"), None, None),
            P(None, ("group", "row"), "tp", None),
            P(None, ("group", "row"), None),
            P("group"),
            P("group"),
            P(("group", "row")),
        ),
        out_specs=P(None, ("group", "row"), "tp", None),
        check_vma=False,
    )
```

```python
import functools

import jax
import jax.numpy as jnp
from jax import lax
from jax.experimental import pallas as pl
from jax.experimental.pallas import tpu as pltpu
from jax.sharding import PartitionSpec as P

KV_RANK = 512
ROPE_DIM = 64
NOPE_DIM = 128
SPR = 8


def pick(array, index):
    return lax.map(lambda i: lax.dynamic_index_in_dim(array, i, 0, keepdims=False), index)


def shards(prompt_latent, row_cache, queries, new_latent, prompt_len, assign, row_ctx):
    row_count = lax.axis_size("row")
    pair_count = lax.axis_size("tp")
    row_place = lax.axis_index("row")
    rows_here = row_cache.shape[0]
    group_rows = prompt_latent.shape[1]
    piece_len = prompt_latent.shape[2]
    latent_width = prompt_latent.shape[3]
    full_len = piece_len * SPR * pair_count
    most_slots = min(rows_here, max(2, 2 * rows_here * SPR // row_count))
    home_group = row_place // SPR
    dest_prompt = assign.reshape(row_count, rows_here)
    in_group = dest_prompt // group_rows == home_group
    row_ids = jnp.arange(rows_here, dtype=jnp.int32)
    up_to = row_ids[:, None] <= row_ids[None, :]
    rank = jnp.sum((in_group[:, :, None] & up_to[None]).astype(jnp.int32), axis=1) - 1
    slot_ids = jnp.arange(most_slots, dtype=jnp.int32)
    picked = in_group[:, :, None] & (rank[:, :, None] == slot_ids[None, None, :])
    local_id = dest_prompt - home_group * group_rows
    source_index = jnp.sum(jnp.where(picked, local_id[:, :, None], 0), axis=1)
    filled = jnp.any(picked, axis=1).reshape(-1)
    owned = lax.dynamic_slice_in_dim(assign, row_place * rows_here, rows_here)
    owned_group = owned // group_rows
    same_before = (owned_group[:, None] == owned_group[None, :]) & (
        row_ids[None, :] < row_ids[:, None]
    )
    own_rank = jnp.sum(same_before.astype(jnp.int32), axis=1)
    block_ids = jnp.arange(SPR, dtype=jnp.int32)
    fetch_index = (
        (owned_group[:, None] * SPR + block_ids[None, :]) * most_slots + own_rank[:, None]
    ).reshape(-1)
    local = prompt_latent[0]
    rows_taken = pick(local, source_index.reshape(-1))
    rows_taken = jnp.where(filled[:, None, None], rows_taken, jnp.zeros_like(rows_taken))
    moved = lax.all_to_all(
        rows_taken.reshape((row_count, most_slots) + local.shape[1:]),
        "row",
        split_axis=0,
        concat_axis=0,
        tiled=True,
    )
    flat = moved.reshape(row_count * most_slots, piece_len, latent_width)
    mine = pick(flat, fetch_index).reshape(rows_here, SPR, 1, piece_len, latent_width)
    paired = lax.all_gather(mine, "tp", axis=2, tiled=True)
    latents = paired.reshape(rows_here, full_len, latent_width)
    live_len = pick(prompt_len, owned)
    scale_factor = (NOPE_DIM + ROPE_DIM) ** (-0.5)
    steps_count = queries.shape[0]
    cache_len = row_cache.shape[1]
    cache_scores = (
        jnp.einsum("srhc,rkc->rshk", queries, row_cache, preferred_element_type=jnp.float32)
        * scale_factor
    )
    cache_live = jnp.arange(cache_len, dtype=jnp.int32)[None, :] < row_ctx[:, None]
    cache_scores = jnp.where(cache_live[:, None, None, :], cache_scores, -jnp.inf)
    fresh_scores = (
        jnp.einsum("srhc,jrc->rshj", queries, new_latent, preferred_element_type=jnp.float32)
        * scale_factor
    )
    step_ids = jnp.arange(steps_count, dtype=jnp.int32)
    causal = step_ids[None, :] <= step_ids[:, None]
    fresh_scores = jnp.where(causal[None, :, None, :], fresh_scores, -jnp.inf)
    prompt_live = jnp.arange(full_len, dtype=jnp.int32)[None, :] < live_len[:, None]
    prompt_scores = (
        jnp.einsum("srhc,rkc->rshk", queries, latents, preferred_element_type=jnp.float32)
        * scale_factor
    )
    prompt_scores = jnp.where(prompt_live[:, None, None, :], prompt_scores, -jnp.inf)
    row_top = jnp.maximum(
        jnp.max(prompt_scores, axis=3, keepdims=True),
        jnp.maximum(
            jnp.max(cache_scores, axis=3, keepdims=True),
            jnp.max(fresh_scores, axis=3, keepdims=True),
        ),
    )
    prompt_exp = jnp.exp(prompt_scores - row_top)
    cache_exp = jnp.exp(cache_scores - row_top)
    fresh_exp = jnp.exp(fresh_scores - row_top)
    denominator = (
        jnp.sum(prompt_exp, axis=3, keepdims=True)
        + jnp.sum(cache_exp, axis=3, keepdims=True)
        + jnp.sum(fresh_exp, axis=3, keepdims=True)
    )
    prompt_probs = (prompt_exp / denominator).astype(jnp.bfloat16)
    cache_probs = (cache_exp / denominator).astype(jnp.bfloat16)
    fresh_probs = (fresh_exp / denominator).astype(jnp.bfloat16)
    cache_out = jnp.einsum(
        "rshk,rkc->srhc", cache_probs, row_cache[:, :, :KV_RANK], preferred_element_type=jnp.float32
    )
    fresh_out = jnp.einsum(
        "rshj,jrc->srhc",
        fresh_probs,
        new_latent[:, :, :KV_RANK],
        preferred_element_type=jnp.float32,
    )
    prompt_out = jnp.einsum(
        "rshk,rkc->srhc", prompt_probs, latents[:, :, :KV_RANK], preferred_element_type=jnp.float32
    )
    return (prompt_out + cache_out + fresh_out).astype(jnp.bfloat16)


MESH = pl.DeviceIdType.MESH


def flip(index, bits):
    out = index
    place = 1
    while place <= bits:
        if bits & place:
            out = out + place * (1 - 2 * ((index // place) % 2))
        place *= 2
    return out


def fused(
    order,
    scale,
    prompt_hbm,
    cache_hbm,
    query_hbm,
    fresh_hbm,
    plen_ref,
    assign_ref,
    ctx_ref,
    out_ref,
    prompt_v,
    cache_v,
    query_v,
    fresh_v,
    fresh_keys,
    query_rope,
    send,
    recv,
    acc,
    top,
    total,
    load_sem,
    prompt_sem,
    send_sem,
    recv_sem,
    relay_sem,
    relayed_sem,
):
    me = lax.axis_index("row")
    core = lax.axis_index("tp")
    mate = 1 - core
    peers = len(order) + 1
    rows = cache_v.shape[0]
    cache_len = cache_v.shape[2]
    steps, _, heads, width = query_v.shape
    rope = width - KV_RANK
    piece = prompt_v.shape[1]
    block = 2 * piece
    lanes = rows * rope
    queries_n = steps * heads

    loads = [
        pltpu.make_async_copy(source, target, load_sem.at[i])
        for i, (source, target) in enumerate(
            (
                (query_hbm, query_v),
                (cache_hbm, cache_v),
                (fresh_hbm, fresh_v),
            )
        )
    ]
    groups = prompt_v.shape[0] // 4
    prompt_loads = [
        pltpu.make_async_copy(
            prompt_hbm.at[pl.ds(i * groups, groups)],
            prompt_v.at[pl.ds(i * groups, groups)],
            prompt_sem.at[i],
        )
        for i in range(4)
    ]
    for load in prompt_loads:
        load.start()

    barrier = pltpu.get_barrier_semaphore()
    for bits in order:
        pl.semaphore_signal(barrier, inc=1, device_id={"row": flip(me, bits)}, device_id_type=MESH)
    pl.semaphore_signal(barrier, inc=1, device_id={"tp": mate}, device_id_type=MESH)

    fresh_keys[...] = jnp.zeros_like(fresh_keys)
    query_rope[...] = jnp.zeros_like(query_rope)

    for load in prompt_loads:
        load.wait()

    def pack(dest, target):
        tails = []
        for i in range(rows):
            taken = prompt_v[assign_ref[dest * rows + i]]
            target[:, i * KV_RANK : (i + 1) * KV_RANK] = taken[:, :KV_RANK]
            tails.append(taken[:, KV_RANK:])
        target[:, rows * KV_RANK :] = jnp.concatenate(tails, axis=1)

    for bits in order:
        pack(flip(me, bits), send.at[bits])
    pack(me, recv.at[0, core])

    pl.semaphore_wait(barrier, peers)

    final = order[-1]
    early = piece * 3 // 4
    cuts = [(bits, bits, 0, piece) for bits in order[:-1]]
    cuts += [(final, final, 0, early), (final, peers, early, piece - early)]
    sends = []
    for bits, at, first, count in cuts:
        part = pl.ds(first, count)
        copy = pltpu.make_async_remote_copy(
            src_ref=send.at[bits, part],
            dst_ref=recv.at[bits, core, part],
            send_sem=send_sem.at[at],
            recv_sem=recv_sem.at[at],
            device_id={"row": flip(me, bits)},
            device_id_type=MESH,
        )
        copy.start()
        sends.append(copy)
    for load in loads:
        load.start()
    relays = {}
    for bits, at, first, count in [(0, 0, 0, piece)] + cuts:
        part = pl.ds(first, count)
        relays[at] = pltpu.make_async_remote_copy(
            src_ref=recv.at[bits, core, part],
            dst_ref=recv.at[bits, core, part],
            send_sem=relay_sem.at[at],
            recv_sem=relayed_sem.at[at],
            device_id={"tp": mate},
            device_id_type=MESH,
        )
    relays[0].start()

    for load in loads:
        load.wait()
    nt = (((1,), (1,)), ((), ()))

    def dot_nt(a, b):
        return lax.dot_general(a, b, nt, preferred_element_type=jnp.float32)

    def dot_nn(a, b):
        return jnp.dot(a, b, preferred_element_type=jnp.float32)

    def wide(x):
        return jnp.concatenate([x] * (KV_RANK // lanes), axis=1)

    col = lax.broadcasted_iota(jnp.int32, (queries_n, lanes), 1)
    step_of = lax.broadcasted_iota(jnp.int32, (queries_n, lanes), 0) // heads
    live = [plen_ref[assign_ref[me * rows + i]] for i in range(rows)]
    for i in range(rows):
        q = query_v[:, i].reshape(queries_n, width)
        q_nope, q_rope = q[:, :KV_RANK], q[:, KV_RANK:]
        query_rope[i, :, i * rope : (i + 1) * rope] = q_rope
        fresh_keys[i, :steps, :] = fresh_v[:, i, :]
        ctx = ctx_ref[i]
        parts = []
        values = []
        for first in range(0, cache_len, lanes):
            keys = cache_v[i, :, first : first + lanes]
            s = dot_nn(q_nope, keys[:KV_RANK]) + dot_nn(q_rope, keys[KV_RANK:])
            parts.append(jnp.where(col + first < ctx, s * scale, -jnp.inf))
            values.append(keys[:KV_RANK])
        keys = fresh_keys[i]
        s = dot_nt(q_nope, keys[:, :KV_RANK]) + dot_nt(q_rope, keys[:, KV_RANK:])
        parts.append(jnp.where(col <= step_of, s * scale, -jnp.inf))
        peak = parts[0]
        for s in parts[1:]:
            peak = jnp.maximum(peak, s)
        peak = jnp.broadcast_to(jnp.max(peak, axis=1, keepdims=True), (queries_n, lanes))
        top[i] = peak
        weights = [jnp.exp(s - peak) for s in parts]
        total[i] = sum(weights[1:], weights[0])
        out = dot_nn(weights[-1].astype(jnp.bfloat16), keys[:, :KV_RANK])
        for w, v in zip(weights, values):
            out = out + dot_nt(w.astype(jnp.bfloat16), v)
        acc[i] = out

    def take_in(bits, between=None):
        limit = flip(me, bits) * block
        for i in range(rows):
            if i == 1 and between is not None:
                between()
            keys = recv[bits].reshape(block, rows * KV_RANK + lanes)
            q_nope = query_v[:, i].reshape(queries_n, width)[:, :KV_RANK]
            v = keys[:, i * KV_RANK : (i + 1) * KV_RANK]
            s = dot_nt(q_nope, v) + dot_nt(query_rope[i], keys[:, rows * KV_RANK :])
            s = jnp.where(col < live[i] - limit, s * scale, -jnp.inf)
            old = top[i]
            peak = jnp.maximum(old, jnp.max(s, axis=1, keepdims=True))
            shrink = jnp.exp(old - peak)
            w = jnp.exp(s - peak)
            top[i] = peak
            total[i] = total[i] * shrink + w
            acc[i] = acc[i] * wide(shrink) + dot_nn(w.astype(jnp.bfloat16), v)

    def take_half(bits, half, last):
        limit = flip(me, bits) * block + half * piece
        for i in range(rows):
            keys = recv[bits, half]
            q_nope = query_v[:, i].reshape(queries_n, width)[:, :KV_RANK]
            v = keys[:, i * KV_RANK : (i + 1) * KV_RANK]
            s = dot_nt(q_nope, v) + dot_nt(query_rope[i], keys[:, rows * KV_RANK :])
            s = jnp.where(col[:, :piece] < live[i] - limit, s * scale, -jnp.inf)
            old = top[i]
            peak = jnp.maximum(old, jnp.max(s, axis=1, keepdims=True))
            shrink = jnp.exp(old - peak)
            w = jnp.exp(s - peak[:, :piece])
            mixed = acc[i] * wide(shrink) + dot_nn(w.astype(jnp.bfloat16), v)
            if last:
                mass = jnp.sum(total[i] * shrink, axis=1, keepdims=True)
                mass = mass + jnp.sum(w, axis=1, keepdims=True)
                mixed = (mixed * (1.0 / mass)).astype(out_ref.dtype)
                out_ref[:, i] = mixed.reshape(steps, heads, KV_RANK)
            else:
                top[i] = peak
                total[i] = total[i] * shrink
                total[i, :, :piece] += w
                acc[i] = mixed

    relays[0].wait_recv()
    take_in(0)
    before = None
    for bits, copy in zip(order[:-1], sends):
        copy.wait_recv()
        relays[bits].start()
        if before is not None:
            relays[before].wait_recv()
            take_in(before)
        before = bits

    def hand_over_last():
        for at, copy in zip((final, peers), sends[-2:]):
            copy.wait_recv()
            relays[at].start()

    relays[before].wait_recv()
    take_in(before, hand_over_last)
    take_half(final, core, False)
    for at in (final, peers):
        relays[at].wait_recv()
    take_half(final, mate, True)
    for copy in sends:
        copy.wait_send()
    for relay in relays.values():
        relay.wait_send()


def direct(prompt_latent, row_cache, queries, new_latent, prompt_len, assign, row_ctx):
    peers = lax.axis_size("row")
    order = (1, 2, 3) + tuple(range(4, peers))
    steps, rows, heads, width = queries.shape
    rope = width - KV_RANK
    local = prompt_latent.reshape(prompt_latent.shape[1:])
    cache_t = jnp.swapaxes(row_cache, 1, 2)
    piece = local.shape[1]
    lanes = rows * rope
    packed = rows * KV_RANK + lanes
    total_n = steps * heads
    bf16, f32 = jnp.bfloat16, jnp.float32
    hbm = pl.BlockSpec(memory_space=pl.ANY)
    smem = pl.BlockSpec(memory_space=pltpu.SMEM)
    return pl.pallas_call(
        functools.partial(fused, order, (NOPE_DIM + ROPE_DIM) ** (-0.5)),
        out_shape=pltpu.VMEM((steps, rows, heads, KV_RANK), bf16),
        in_specs=[hbm, hbm, hbm, hbm, smem, smem, smem],
        out_specs=pl.BlockSpec(memory_space=pltpu.VMEM),
        scratch_shapes=[
            pltpu.VMEM(local.shape, bf16),
            pltpu.VMEM(cache_t.shape, bf16),
            pltpu.VMEM(queries.shape, bf16),
            pltpu.VMEM(new_latent.shape, bf16),
            pltpu.VMEM((rows, lanes, width), bf16),
            pltpu.VMEM((rows, total_n, lanes), bf16),
            pltpu.VMEM((peers, piece, packed), bf16),
            pltpu.VMEM((peers, 2, piece, packed), bf16),
            pltpu.VMEM((rows, total_n, KV_RANK), f32),
            pltpu.VMEM((rows, total_n, lanes), f32),
            pltpu.VMEM((rows, total_n, lanes), f32),
            pltpu.SemaphoreType.DMA((3,)),
            pltpu.SemaphoreType.DMA((4,)),
            pltpu.SemaphoreType.DMA((peers + 1,)),
            pltpu.SemaphoreType.DMA((peers + 1,)),
            pltpu.SemaphoreType.DMA((peers + 1,)),
            pltpu.SemaphoreType.DMA((peers + 1,)),
        ],
        compiler_params=pltpu.CompilerParams(collective_id=0, has_side_effects=True),
    )(local, cache_t, queries, new_latent, prompt_len, assign, row_ctx)


def solution(mesh):
    one_group = mesh.shape["row"] == SPR and mesh.shape["tp"] == 2
    return jax.shard_map(
        direct if one_group else shards,
        mesh=mesh,
        in_specs=(
            P(("group", "row"), None, "tp", None),
            P(("group", "row"), None, None),
            P(None, ("group", "row"), "tp", None),
            P(None, ("group", "row"), None),
            P("group"),
            P("group"),
            P(("group", "row")),
        ),
        out_specs=P(None, ("group", "row"), "tp", None),
        check_vma=False,
    )
```

```python
import functools

import jax
import jax.numpy as jnp
from jax import lax
from jax.experimental import pallas as pl
from jax.experimental.pallas import tpu as pltpu
from jax.sharding import PartitionSpec as P

KV_RANK = 512
ROPE_DIM = 64
NOPE_DIM = 128
SPR = 8


def pick(array, index):
    return lax.map(lambda i: lax.dynamic_index_in_dim(array, i, 0, keepdims=False), index)


def shards(prompt_latent, row_cache, queries, new_latent, prompt_len, assign, row_ctx):
    row_count = lax.axis_size("row")
    pair_count = lax.axis_size("tp")
    row_place = lax.axis_index("row")
    rows_here = row_cache.shape[0]
    group_rows = prompt_latent.shape[1]
    piece_len = prompt_latent.shape[2]
    latent_width = prompt_latent.shape[3]
    full_len = piece_len * SPR * pair_count
    most_slots = min(rows_here, max(2, 2 * rows_here * SPR // row_count))
    home_group = row_place // SPR
    dest_prompt = assign.reshape(row_count, rows_here)
    in_group = dest_prompt // group_rows == home_group
    row_ids = jnp.arange(rows_here, dtype=jnp.int32)
    up_to = row_ids[:, None] <= row_ids[None, :]
    rank = jnp.sum((in_group[:, :, None] & up_to[None]).astype(jnp.int32), axis=1) - 1
    slot_ids = jnp.arange(most_slots, dtype=jnp.int32)
    picked = in_group[:, :, None] & (rank[:, :, None] == slot_ids[None, None, :])
    local_id = dest_prompt - home_group * group_rows
    source_index = jnp.sum(jnp.where(picked, local_id[:, :, None], 0), axis=1)
    filled = jnp.any(picked, axis=1).reshape(-1)
    owned = lax.dynamic_slice_in_dim(assign, row_place * rows_here, rows_here)
    owned_group = owned // group_rows
    same_before = (owned_group[:, None] == owned_group[None, :]) & (
        row_ids[None, :] < row_ids[:, None]
    )
    own_rank = jnp.sum(same_before.astype(jnp.int32), axis=1)
    block_ids = jnp.arange(SPR, dtype=jnp.int32)
    fetch_index = (
        (owned_group[:, None] * SPR + block_ids[None, :]) * most_slots + own_rank[:, None]
    ).reshape(-1)
    local = prompt_latent[0]
    rows_taken = pick(local, source_index.reshape(-1))
    rows_taken = jnp.where(filled[:, None, None], rows_taken, jnp.zeros_like(rows_taken))
    moved = lax.all_to_all(
        rows_taken.reshape((row_count, most_slots) + local.shape[1:]),
        "row",
        split_axis=0,
        concat_axis=0,
        tiled=True,
    )
    flat = moved.reshape(row_count * most_slots, piece_len, latent_width)
    mine = pick(flat, fetch_index).reshape(rows_here, SPR, 1, piece_len, latent_width)
    paired = lax.all_gather(mine, "tp", axis=2, tiled=True)
    latents = paired.reshape(rows_here, full_len, latent_width)
    live_len = pick(prompt_len, owned)
    scale_factor = (NOPE_DIM + ROPE_DIM) ** (-0.5)
    steps_count = queries.shape[0]
    cache_len = row_cache.shape[1]
    cache_scores = (
        jnp.einsum("srhc,rkc->rshk", queries, row_cache, preferred_element_type=jnp.float32)
        * scale_factor
    )
    cache_live = jnp.arange(cache_len, dtype=jnp.int32)[None, :] < row_ctx[:, None]
    cache_scores = jnp.where(cache_live[:, None, None, :], cache_scores, -jnp.inf)
    fresh_scores = (
        jnp.einsum("srhc,jrc->rshj", queries, new_latent, preferred_element_type=jnp.float32)
        * scale_factor
    )
    step_ids = jnp.arange(steps_count, dtype=jnp.int32)
    causal = step_ids[None, :] <= step_ids[:, None]
    fresh_scores = jnp.where(causal[None, :, None, :], fresh_scores, -jnp.inf)
    prompt_live = jnp.arange(full_len, dtype=jnp.int32)[None, :] < live_len[:, None]
    prompt_scores = (
        jnp.einsum("srhc,rkc->rshk", queries, latents, preferred_element_type=jnp.float32)
        * scale_factor
    )
    prompt_scores = jnp.where(prompt_live[:, None, None, :], prompt_scores, -jnp.inf)
    row_top = jnp.maximum(
        jnp.max(prompt_scores, axis=3, keepdims=True),
        jnp.maximum(
            jnp.max(cache_scores, axis=3, keepdims=True),
            jnp.max(fresh_scores, axis=3, keepdims=True),
        ),
    )
    prompt_exp = jnp.exp(prompt_scores - row_top)
    cache_exp = jnp.exp(cache_scores - row_top)
    fresh_exp = jnp.exp(fresh_scores - row_top)
    denominator = (
        jnp.sum(prompt_exp, axis=3, keepdims=True)
        + jnp.sum(cache_exp, axis=3, keepdims=True)
        + jnp.sum(fresh_exp, axis=3, keepdims=True)
    )
    prompt_probs = (prompt_exp / denominator).astype(jnp.bfloat16)
    cache_probs = (cache_exp / denominator).astype(jnp.bfloat16)
    fresh_probs = (fresh_exp / denominator).astype(jnp.bfloat16)
    cache_out = jnp.einsum(
        "rshk,rkc->srhc", cache_probs, row_cache[:, :, :KV_RANK], preferred_element_type=jnp.float32
    )
    fresh_out = jnp.einsum(
        "rshj,jrc->srhc",
        fresh_probs,
        new_latent[:, :, :KV_RANK],
        preferred_element_type=jnp.float32,
    )
    prompt_out = jnp.einsum(
        "rshk,rkc->srhc", prompt_probs, latents[:, :, :KV_RANK], preferred_element_type=jnp.float32
    )
    return (prompt_out + cache_out + fresh_out).astype(jnp.bfloat16)


MESH = pl.DeviceIdType.MESH


LEVELS = (1, 0, 0, 2)
SENDS = (
    ((2, 0), (2, 1), (1, 0), (1, 1), (0, 1), (3, 0), (3, 1)),
    ((2, 0), (2, 1), (1, 1), (0, 0), (0, 1), (3, 0), (3, 1)),
    ((1, 1), (0, 1), (0, 0), (1, 0), (2, 1), (3, 0), (3, 1)),
    ((1, 0), (1, 1), (2, 0), (2, 1), (0, 0), (0, 1), (3, 1)),
)
TAKES = (
    ((0, 1), (1, 0), (1, 1), (2, 1), (3, 0), (3, 1), (2, 0)),
    ((1, 1), (3, 0), (3, 1), (2, 1), (0, 0), (0, 1), (2, 0)),
    ((0, 0), (0, 1), (2, 1), (1, 0), (3, 0), (3, 1), (1, 1)),
    ((3, 1), (2, 0), (2, 1), (0, 0), (0, 1), (1, 0), (1, 1)),
)


def by_rank(rank, a, b, c, d):
    high, low = rank // 2, rank % 2
    return (1 - high) * ((1 - low) * a + low * b) + high * ((1 - low) * c + low * d)


def peers_of(me, table):
    rank, side = me // 2, me % 2
    found = []
    for step in zip(*table):
        other = by_rank(rank, *(entry[1] for entry in step))
        found.append(2 * by_rank(rank, *(entry[0] for entry in step)) + side + other - 2 * side * other)
    return found


def fused(
    scale,
    prompt_hbm,
    cache_hbm,
    query_hbm,
    fresh_hbm,
    plen_ref,
    assign_ref,
    ctx_ref,
    out_ref,
    prompt_v,
    cache_v,
    query_v,
    fresh_v,
    fresh_keys,
    query_rope,
    send,
    recv,
    acc,
    top,
    total,
    load_sem,
    prompt_sem,
    send_sem,
    recv_sem,
    relay_sem,
    relayed_sem,
    ready,
):
    me = lax.axis_index("row")
    core = lax.axis_index("tp")
    mate = 1 - core
    targets, sources = peers_of(me, SENDS), peers_of(me, TAKES)
    peers = len(targets) + 1
    rows = cache_v.shape[0]
    cache_len = cache_v.shape[2]
    steps, _, heads, width = query_v.shape
    rope = width - KV_RANK
    piece = prompt_v.shape[1]
    block = 2 * piece
    lanes = rows * rope
    queries_n = steps * heads

    loads = [
        pltpu.make_async_copy(source, target, load_sem.at[i])
        for i, (source, target) in enumerate(
            (
                (query_hbm, query_v),
                (cache_hbm, cache_v),
                (fresh_hbm, fresh_v),
            )
        )
    ]
    groups = prompt_v.shape[0] // 4
    prompt_loads = [
        pltpu.make_async_copy(
            prompt_hbm.at[pl.ds(i * groups, groups)],
            prompt_v.at[pl.ds(i * groups, groups)],
            prompt_sem.at[i],
        )
        for i in range(4)
    ]
    for load in prompt_loads:
        load.start()

    barrier = pltpu.get_barrier_semaphore()

    def tell(semaphore, row):
        pl.semaphore_signal(semaphore, inc=1, device_id={"row": row}, device_id_type=MESH)

    pl.semaphore_signal(barrier, inc=1, device_id={"tp": mate}, device_id_type=MESH)
    level = by_rank(me // 2, *LEVELS)
    row_levels = [LEVELS[row // 2] for row in range(peers)]
    for row, its in enumerate(row_levels):

        @pl.when((row != me) & (its >= level))
        def _():
            tell(barrier, row)

    pl.semaphore_wait(barrier, by_rank(me // 2, *(sum(its <= LEVELS[r] for its in row_levels) for r in range(4))))
    for row, its in enumerate(row_levels):

        @pl.when(its < level)
        def _():
            tell(ready.at[me], row)

    for load in prompt_loads:
        load.wait()

    def pack(dest, target):
        tails = []
        for i in range(rows):
            taken = prompt_v[assign_ref[dest * rows + i]]
            target[:, i * KV_RANK : (i + 1) * KV_RANK] = taken[:, :KV_RANK]
            tails.append(taken[:, KV_RANK:])
        target[:, rows * KV_RANK :] = jnp.concatenate(tails, axis=1)

    early = piece * 3 // 4
    cuts = [pl.ds(0, early), pl.ds(early, piece - early)]
    whole = pl.ds(0, piece)

    def copy_to(step, target, source, cut):
        return pltpu.make_async_remote_copy(
            src_ref=send.at[step, cuts[cut]],
            dst_ref=recv.at[source, core, cuts[cut]],
            send_sem=send_sem.at[step, cut],
            recv_sem=recv_sem.at[source, cut],
            device_id={"row": target},
            device_id_type=MESH,
        )

    def relay_of(step, source, part):
        return pltpu.make_async_remote_copy(
            src_ref=recv.at[source, core, part],
            dst_ref=recv.at[source, core, part],
            send_sem=relay_sem.at[step],
            recv_sem=relayed_sem.at[step],
            device_id={"tp": mate},
            device_id_type=MESH,
        )

    sends = []
    for step, target in enumerate(targets):
        pack(target, send.at[step])

        @pl.when(by_rank(target // 2, *LEVELS) > level)
        def _():
            pl.semaphore_wait(ready.at[target], 1)

        for cut in range(2):
            copy = copy_to(step, target, me, cut)
            copy.start()
            sends.append(copy)
    for load in loads:
        load.start()
    arrivals = [[copy_to(step, source, source, cut) for cut in range(2)] for step, source in enumerate(sources)]
    relays = [relay_of(step, source, whole) for step, source in enumerate(sources[:-1])]
    relays += [relay_of(peers - 2 + cut, sources[-1], cuts[cut]) for cut in range(2)]
    own_relay = relay_of(peers, me, whole)
    pack(me, recv.at[me, core])
    own_relay.start()
    fresh_keys[...] = jnp.zeros_like(fresh_keys)
    query_rope[...] = jnp.zeros_like(query_rope)

    for load in loads:
        load.wait()
    nt = (((1,), (1,)), ((), ()))

    def dot_nt(a, b):
        return lax.dot_general(a, b, nt, preferred_element_type=jnp.float32)

    def dot_nn(a, b):
        return jnp.dot(a, b, preferred_element_type=jnp.float32)

    def wide(x):
        return jnp.concatenate([x] * (KV_RANK // lanes), axis=1)

    col = lax.broadcasted_iota(jnp.int32, (queries_n, lanes), 1)
    step_of = lax.broadcasted_iota(jnp.int32, (queries_n, lanes), 0) // heads
    live = [plen_ref[assign_ref[me * rows + i]] for i in range(rows)]
    for i in range(rows):
        q = query_v[:, i].reshape(queries_n, width)
        q_nope, q_rope = q[:, :KV_RANK], q[:, KV_RANK:]
        query_rope[i, :, i * rope : (i + 1) * rope] = q_rope
        fresh_keys[i, :steps, :] = fresh_v[:, i, :]
        ctx = ctx_ref[i]
        parts = []
        values = []
        for first in range(0, cache_len, lanes):
            keys = cache_v[i, :, first : first + lanes]
            s = dot_nn(q_nope, keys[:KV_RANK]) + dot_nn(q_rope, keys[KV_RANK:])
            parts.append(jnp.where(col + first < ctx, s * scale, -jnp.inf))
            values.append(keys[:KV_RANK])
        keys = fresh_keys[i]
        s = dot_nt(q_nope, keys[:, :KV_RANK]) + dot_nt(q_rope, keys[:, KV_RANK:])
        parts.append(jnp.where(col <= step_of, s * scale, -jnp.inf))
        peak = parts[0]
        for s in parts[1:]:
            peak = jnp.maximum(peak, s)
        peak = jnp.broadcast_to(jnp.max(peak, axis=1, keepdims=True), (queries_n, lanes))
        top[i] = peak
        weights = [jnp.exp(s - peak) for s in parts]
        total[i] = sum(weights[1:], weights[0])
        out = dot_nn(weights[-1].astype(jnp.bfloat16), keys[:, :KV_RANK])
        for w, v in zip(weights, values):
            out = out + dot_nt(w.astype(jnp.bfloat16), v)
        acc[i] = out

    def take_in(source):
        limit = source * block
        for i in range(rows):
            keys = recv[source].reshape(block, rows * KV_RANK + lanes)
            q_nope = query_v[:, i].reshape(queries_n, width)[:, :KV_RANK]
            v = keys[:, i * KV_RANK : (i + 1) * KV_RANK]
            s = dot_nt(q_nope, v) + dot_nt(query_rope[i], keys[:, rows * KV_RANK :])
            s = jnp.where(col < live[i] - limit, s * scale, -jnp.inf)
            old = top[i]
            peak = jnp.maximum(old, jnp.max(s, axis=1, keepdims=True))
            shrink = jnp.exp(old - peak)
            w = jnp.exp(s - peak)
            top[i] = peak
            total[i] = total[i] * shrink + w
            acc[i] = acc[i] * wide(shrink) + dot_nn(w.astype(jnp.bfloat16), v)

    def take_half(source, half, last):
        limit = source * block + half * piece
        for i in range(rows):
            keys = recv[source, half]
            q_nope = query_v[:, i].reshape(queries_n, width)[:, :KV_RANK]
            v = keys[:, i * KV_RANK : (i + 1) * KV_RANK]
            s = dot_nt(q_nope, v) + dot_nt(query_rope[i], keys[:, rows * KV_RANK :])
            s = jnp.where(col[:, :piece] < live[i] - limit, s * scale, -jnp.inf)
            old = top[i]
            peak = jnp.maximum(old, jnp.max(s, axis=1, keepdims=True))
            shrink = jnp.exp(old - peak)
            w = jnp.exp(s - peak[:, :piece])
            mixed = acc[i] * wide(shrink) + dot_nn(w.astype(jnp.bfloat16), v)
            if last:
                mass = jnp.sum(total[i] * shrink, axis=1, keepdims=True)
                mass = mass + jnp.sum(w, axis=1, keepdims=True)
                mixed = (mixed * (1.0 / mass)).astype(out_ref.dtype)
                out_ref[:, i] = mixed.reshape(steps, heads, KV_RANK)
            else:
                top[i] = peak
                total[i] = total[i] * shrink
                total[i, :, :piece] += w
                acc[i] = mixed

    own_relay.wait_recv()
    take_in(me)
    for step in range(peers - 2):
        for arrival in arrivals[step]:
            arrival.wait_recv()
        relays[step].start()
        if step:
            relays[step - 1].wait_recv()
            take_in(sources[step - 1])
    relays[peers - 3].wait_recv()
    take_in(sources[-2])
    for arrival, relay in zip(arrivals[-1], relays[-2:]):
        arrival.wait_recv()
        relay.start()
    take_half(sources[-1], core, False)
    for relay in relays[-2:]:
        relay.wait_recv()
    take_half(sources[-1], mate, True)
    for copy in sends:
        copy.wait_send()
    for relay in relays + [own_relay]:
        relay.wait_send()


def direct(prompt_latent, row_cache, queries, new_latent, prompt_len, assign, row_ctx):
    peers = lax.axis_size("row")
    steps, rows, heads, width = queries.shape
    rope = width - KV_RANK
    local = prompt_latent.reshape(prompt_latent.shape[1:])
    cache_t = jnp.swapaxes(row_cache, 1, 2)
    piece = local.shape[1]
    lanes = rows * rope
    packed = rows * KV_RANK + lanes
    total_n = steps * heads
    bf16, f32 = jnp.bfloat16, jnp.float32
    hbm = pl.BlockSpec(memory_space=pl.ANY)
    smem = pl.BlockSpec(memory_space=pltpu.SMEM)
    return pl.pallas_call(
        functools.partial(fused, (NOPE_DIM + ROPE_DIM) ** (-0.5)),
        out_shape=pltpu.VMEM((steps, rows, heads, KV_RANK), bf16),
        in_specs=[hbm, hbm, hbm, hbm, smem, smem, smem],
        out_specs=pl.BlockSpec(memory_space=pltpu.VMEM),
        scratch_shapes=[
            pltpu.VMEM(local.shape, bf16),
            pltpu.VMEM(cache_t.shape, bf16),
            pltpu.VMEM(queries.shape, bf16),
            pltpu.VMEM(new_latent.shape, bf16),
            pltpu.VMEM((rows, lanes, width), bf16),
            pltpu.VMEM((rows, total_n, lanes), bf16),
            pltpu.VMEM((peers - 1, piece, packed), bf16),
            pltpu.VMEM((peers, 2, piece, packed), bf16),
            pltpu.VMEM((rows, total_n, KV_RANK), f32),
            pltpu.VMEM((rows, total_n, lanes), f32),
            pltpu.VMEM((rows, total_n, lanes), f32),
            pltpu.SemaphoreType.DMA((3,)),
            pltpu.SemaphoreType.DMA((4,)),
            pltpu.SemaphoreType.DMA((peers - 1, 2)),
            pltpu.SemaphoreType.DMA((peers, 2)),
            pltpu.SemaphoreType.DMA((peers + 1,)),
            pltpu.SemaphoreType.DMA((peers + 1,)),
            pltpu.SemaphoreType.REGULAR((peers,)),
        ],
        compiler_params=pltpu.CompilerParams(collective_id=0, has_side_effects=True),
    )(local, cache_t, queries, new_latent, prompt_len, assign, row_ctx)


def solution(mesh):
    one_group = mesh.shape["row"] == SPR and mesh.shape["tp"] == 2
    return jax.shard_map(
        direct if one_group else shards,
        mesh=mesh,
        in_specs=(
            P(("group", "row"), None, "tp", None),
            P(("group", "row"), None, None),
            P(None, ("group", "row"), "tp", None),
            P(None, ("group", "row"), None),
            P("group"),
            P("group"),
            P(("group", "row")),
        ),
        out_specs=P(None, ("group", "row"), "tp", None),
        check_vma=False,
    )
```

```python
import functools

import jax
import jax.numpy as jnp
from jax import lax
from jax.experimental import pallas as pl
from jax.experimental.pallas import tpu as pltpu
from jax.sharding import PartitionSpec as P

KV_RANK = 512
ROPE_DIM = 64
NOPE_DIM = 128
SPR = 8


def pick(array, index):
    return lax.map(lambda i: lax.dynamic_index_in_dim(array, i, 0, keepdims=False), index)


def shards(prompt_latent, row_cache, queries, new_latent, prompt_len, assign, row_ctx):
    row_count = lax.axis_size("row")
    pair_count = lax.axis_size("tp")
    row_place = lax.axis_index("row")
    rows_here = row_cache.shape[0]
    group_rows = prompt_latent.shape[1]
    piece_len = prompt_latent.shape[2]
    latent_width = prompt_latent.shape[3]
    full_len = piece_len * SPR * pair_count
    most_slots = min(rows_here, max(2, 2 * rows_here * SPR // row_count))
    home_group = row_place // SPR
    dest_prompt = assign.reshape(row_count, rows_here)
    in_group = dest_prompt // group_rows == home_group
    row_ids = jnp.arange(rows_here, dtype=jnp.int32)
    up_to = row_ids[:, None] <= row_ids[None, :]
    rank = jnp.sum((in_group[:, :, None] & up_to[None]).astype(jnp.int32), axis=1) - 1
    slot_ids = jnp.arange(most_slots, dtype=jnp.int32)
    picked = in_group[:, :, None] & (rank[:, :, None] == slot_ids[None, None, :])
    local_id = dest_prompt - home_group * group_rows
    source_index = jnp.sum(jnp.where(picked, local_id[:, :, None], 0), axis=1)
    filled = jnp.any(picked, axis=1).reshape(-1)
    owned = lax.dynamic_slice_in_dim(assign, row_place * rows_here, rows_here)
    owned_group = owned // group_rows
    same_before = (owned_group[:, None] == owned_group[None, :]) & (
        row_ids[None, :] < row_ids[:, None]
    )
    own_rank = jnp.sum(same_before.astype(jnp.int32), axis=1)
    block_ids = jnp.arange(SPR, dtype=jnp.int32)
    fetch_index = (
        (owned_group[:, None] * SPR + block_ids[None, :]) * most_slots + own_rank[:, None]
    ).reshape(-1)
    local = prompt_latent[0]
    rows_taken = pick(local, source_index.reshape(-1))
    rows_taken = jnp.where(filled[:, None, None], rows_taken, jnp.zeros_like(rows_taken))
    moved = lax.all_to_all(
        rows_taken.reshape((row_count, most_slots) + local.shape[1:]),
        "row",
        split_axis=0,
        concat_axis=0,
        tiled=True,
    )
    flat = moved.reshape(row_count * most_slots, piece_len, latent_width)
    mine = pick(flat, fetch_index).reshape(rows_here, SPR, 1, piece_len, latent_width)
    paired = lax.all_gather(mine, "tp", axis=2, tiled=True)
    latents = paired.reshape(rows_here, full_len, latent_width)
    live_len = pick(prompt_len, owned)
    scale_factor = (NOPE_DIM + ROPE_DIM) ** (-0.5)
    steps_count = queries.shape[0]
    cache_len = row_cache.shape[1]
    cache_scores = (
        jnp.einsum("srhc,rkc->rshk", queries, row_cache, preferred_element_type=jnp.float32)
        * scale_factor
    )
    cache_live = jnp.arange(cache_len, dtype=jnp.int32)[None, :] < row_ctx[:, None]
    cache_scores = jnp.where(cache_live[:, None, None, :], cache_scores, -jnp.inf)
    fresh_scores = (
        jnp.einsum("srhc,jrc->rshj", queries, new_latent, preferred_element_type=jnp.float32)
        * scale_factor
    )
    step_ids = jnp.arange(steps_count, dtype=jnp.int32)
    causal = step_ids[None, :] <= step_ids[:, None]
    fresh_scores = jnp.where(causal[None, :, None, :], fresh_scores, -jnp.inf)
    prompt_live = jnp.arange(full_len, dtype=jnp.int32)[None, :] < live_len[:, None]
    prompt_scores = (
        jnp.einsum("srhc,rkc->rshk", queries, latents, preferred_element_type=jnp.float32)
        * scale_factor
    )
    prompt_scores = jnp.where(prompt_live[:, None, None, :], prompt_scores, -jnp.inf)
    row_top = jnp.maximum(
        jnp.max(prompt_scores, axis=3, keepdims=True),
        jnp.maximum(
            jnp.max(cache_scores, axis=3, keepdims=True),
            jnp.max(fresh_scores, axis=3, keepdims=True),
        ),
    )
    prompt_exp = jnp.exp(prompt_scores - row_top)
    cache_exp = jnp.exp(cache_scores - row_top)
    fresh_exp = jnp.exp(fresh_scores - row_top)
    denominator = (
        jnp.sum(prompt_exp, axis=3, keepdims=True)
        + jnp.sum(cache_exp, axis=3, keepdims=True)
        + jnp.sum(fresh_exp, axis=3, keepdims=True)
    )
    prompt_probs = (prompt_exp / denominator).astype(jnp.bfloat16)
    cache_probs = (cache_exp / denominator).astype(jnp.bfloat16)
    fresh_probs = (fresh_exp / denominator).astype(jnp.bfloat16)
    cache_out = jnp.einsum(
        "rshk,rkc->srhc", cache_probs, row_cache[:, :, :KV_RANK], preferred_element_type=jnp.float32
    )
    fresh_out = jnp.einsum(
        "rshj,jrc->srhc",
        fresh_probs,
        new_latent[:, :, :KV_RANK],
        preferred_element_type=jnp.float32,
    )
    prompt_out = jnp.einsum(
        "rshk,rkc->srhc", prompt_probs, latents[:, :, :KV_RANK], preferred_element_type=jnp.float32
    )
    return (prompt_out + cache_out + fresh_out).astype(jnp.bfloat16)


MESH = pl.DeviceIdType.MESH


LEVELS = (1, 0, 0, 2)
SENDS = (
    (4, 5, 2, 3, 1, 6, 7),
    (5, 4, 3, 2, 0, 7, 6),
    (4, 5, 3, 0, 1, 6, 7),
    (5, 4, 2, 1, 0, 7, 6),
    (3, 0, 1, 2, 5, 6, 7),
    (2, 0, 1, 3, 4, 7, 6),
    (2, 3, 4, 5, 0, 1, 7),
    (3, 2, 5, 4, 1, 0, 6),
)
TAKES = (
    (1, 2, 3, 4, 5, 6, 7),
    (0, 3, 2, 7, 6, 5, 4),
    (3, 6, 7, 5, 0, 1, 4),
    (2, 7, 6, 4, 1, 0, 5),
    (0, 1, 5, 2, 6, 7, 3),
    (1, 0, 4, 3, 7, 6, 2),
    (7, 4, 5, 0, 1, 2, 3),
    (6, 5, 4, 1, 0, 3, 2),
)
TOGETHER = (1,)


def by_rank(rank, a, b, c, d):
    high, low = rank // 2, rank % 2
    return (1 - high) * ((1 - low) * a + low * b) + high * ((1 - low) * c + low * d)


def peers_of(me, table):
    rank, side = me // 2, me % 2
    return [(1 - side) * by_rank(rank, *step[::2]) + side * by_rank(rank, *step[1::2]) for step in zip(*table)]


def fused(
    scale,
    prompt_hbm,
    cache_hbm,
    query_hbm,
    fresh_hbm,
    plen_ref,
    assign_ref,
    ctx_ref,
    out_ref,
    prompt_v,
    cache_v,
    query_v,
    fresh_v,
    fresh_keys,
    query_rope,
    send,
    recv,
    acc,
    top,
    total,
    load_sem,
    prompt_sem,
    send_sem,
    recv_sem,
    relay_sem,
    relayed_sem,
    ready,
):
    me = lax.axis_index("row")
    core = lax.axis_index("tp")
    mate = 1 - core
    targets, sources = peers_of(me, SENDS), peers_of(me, TAKES)
    peers = len(targets) + 1
    rows = cache_v.shape[0]
    cache_len = cache_v.shape[2]
    steps, _, heads, width = query_v.shape
    rope = width - KV_RANK
    piece = prompt_v.shape[1]
    block = 2 * piece
    lanes = rows * rope
    queries_n = steps * heads

    loads = [
        pltpu.make_async_copy(source, target, load_sem.at[i])
        for i, (source, target) in enumerate(
            (
                (query_hbm, query_v),
                (cache_hbm, cache_v),
                (fresh_hbm, fresh_v),
            )
        )
    ]
    groups = prompt_v.shape[0] // 4
    prompt_loads = [
        pltpu.make_async_copy(
            prompt_hbm.at[pl.ds(i * groups, groups)],
            prompt_v.at[pl.ds(i * groups, groups)],
            prompt_sem.at[i],
        )
        for i in range(4)
    ]
    for load in prompt_loads:
        load.start()

    barrier = pltpu.get_barrier_semaphore()

    def tell(semaphore, row):
        pl.semaphore_signal(semaphore, inc=1, device_id={"row": row}, device_id_type=MESH)

    pl.semaphore_signal(barrier, inc=1, device_id={"tp": mate}, device_id_type=MESH)
    level = by_rank(me // 2, *LEVELS)
    row_levels = [LEVELS[row // 2] for row in range(peers)]
    for row, its in enumerate(row_levels):

        @pl.when((row != me) & (its >= level))
        def _():
            tell(barrier, row)

    pl.semaphore_wait(barrier, by_rank(me // 2, *(sum(its <= LEVELS[r] for its in row_levels) for r in range(4))))
    for row, its in enumerate(row_levels):

        @pl.when(its < level)
        def _():
            tell(ready.at[me], row)

    for load in prompt_loads:
        load.wait()

    def pack(dest, target):
        tails = []
        for i in range(rows):
            taken = prompt_v[assign_ref[dest * rows + i]]
            target[:, i * KV_RANK : (i + 1) * KV_RANK] = taken[:, :KV_RANK]
            tails.append(taken[:, KV_RANK:])
        target[:, rows * KV_RANK :] = jnp.concatenate(tails, axis=1)

    early = piece * 3 // 4
    cuts = [pl.ds(0, early), pl.ds(early, piece - early)]
    whole = pl.ds(0, piece)

    def copy_to(step, target, source, cut):
        return pltpu.make_async_remote_copy(
            src_ref=send.at[step, cuts[cut]],
            dst_ref=recv.at[source, core, cuts[cut]],
            send_sem=send_sem.at[step, cut],
            recv_sem=recv_sem.at[source, cut],
            device_id={"row": target},
            device_id_type=MESH,
        )

    def relay_of(step, source, part):
        return pltpu.make_async_remote_copy(
            src_ref=recv.at[source, core, part],
            dst_ref=recv.at[source, core, part],
            send_sem=relay_sem.at[step],
            recv_sem=relayed_sem.at[step],
            device_id={"tp": mate},
            device_id_type=MESH,
        )

    sends = []
    for step, target in enumerate(targets):
        pack(target, send.at[step])

        @pl.when(by_rank(target // 2, *LEVELS) > level)
        def _():
            pl.semaphore_wait(ready.at[target], 1)

        for cut in range(2):
            copy = copy_to(step, target, me, cut)
            copy.start()
            sends.append(copy)
    for load in loads:
        load.start()
    arrivals = [[copy_to(step, source, source, cut) for cut in range(2)] for step, source in enumerate(sources)]
    relays = [relay_of(step, source, whole) for step, source in enumerate(sources[:-1])]
    relays += [relay_of(peers - 2 + cut, sources[-1], cuts[cut]) for cut in range(2)]
    own_relay = relay_of(peers, me, whole)
    pack(me, recv.at[me, core])
    own_relay.start()
    fresh_keys[...] = jnp.zeros_like(fresh_keys)
    query_rope[...] = jnp.zeros_like(query_rope)

    for load in loads:
        load.wait()
    nt = (((1,), (1,)), ((), ()))

    def dot_nt(a, b):
        return lax.dot_general(a, b, nt, preferred_element_type=jnp.float32)

    def dot_nn(a, b):
        return jnp.dot(a, b, preferred_element_type=jnp.float32)

    def wide(x):
        return jnp.concatenate([x] * (KV_RANK // lanes), axis=1)

    col = lax.broadcasted_iota(jnp.int32, (queries_n, lanes), 1)
    step_of = lax.broadcasted_iota(jnp.int32, (queries_n, lanes), 0) // heads
    live = [plen_ref[assign_ref[me * rows + i]] for i in range(rows)]
    for i in range(rows):
        q = query_v[:, i].reshape(queries_n, width)
        q_nope, q_rope = q[:, :KV_RANK], q[:, KV_RANK:]
        query_rope[i, :, i * rope : (i + 1) * rope] = q_rope
        fresh_keys[i, :steps, :] = fresh_v[:, i, :]
        ctx = ctx_ref[i]
        parts = []
        values = []
        for first in range(0, cache_len, lanes):
            keys = cache_v[i, :, first : first + lanes]
            s = dot_nn(q_nope, keys[:KV_RANK]) + dot_nn(q_rope, keys[KV_RANK:])
            parts.append(jnp.where(col + first < ctx, s * scale, -jnp.inf))
            values.append(keys[:KV_RANK])
        keys = fresh_keys[i]
        s = dot_nt(q_nope, keys[:, :KV_RANK]) + dot_nt(q_rope, keys[:, KV_RANK:])
        parts.append(jnp.where(col <= step_of, s * scale, -jnp.inf))
        peak = parts[0]
        for s in parts[1:]:
            peak = jnp.maximum(peak, s)
        peak = jnp.broadcast_to(jnp.max(peak, axis=1, keepdims=True), (queries_n, lanes))
        top[i] = peak
        weights = [jnp.exp(s - peak) for s in parts]
        total[i] = sum(weights[1:], weights[0])
        out = dot_nn(weights[-1].astype(jnp.bfloat16), keys[:, :KV_RANK])
        for w, v in zip(weights, values):
            out = out + dot_nt(w.astype(jnp.bfloat16), v)
        acc[i] = out

    def take_in(source):
        limit = source * block
        for i in range(rows):
            keys = recv[source].reshape(block, rows * KV_RANK + lanes)
            q_nope = query_v[:, i].reshape(queries_n, width)[:, :KV_RANK]
            v = keys[:, i * KV_RANK : (i + 1) * KV_RANK]
            s = dot_nt(q_nope, v) + dot_nt(query_rope[i], keys[:, rows * KV_RANK :])
            s = jnp.where(col < live[i] - limit, s * scale, -jnp.inf)
            old = top[i]
            peak = jnp.maximum(old, jnp.max(s, axis=1, keepdims=True))
            shrink = jnp.exp(old - peak)
            w = jnp.exp(s - peak)
            top[i] = peak
            total[i] = total[i] * shrink + w
            acc[i] = acc[i] * wide(shrink) + dot_nn(w.astype(jnp.bfloat16), v)

    def take_half(source, half, last):
        limit = source * block + half * piece
        for i in range(rows):
            keys = recv[source, half]
            q_nope = query_v[:, i].reshape(queries_n, width)[:, :KV_RANK]
            v = keys[:, i * KV_RANK : (i + 1) * KV_RANK]
            s = dot_nt(q_nope, v) + dot_nt(query_rope[i], keys[:, rows * KV_RANK :])
            s = jnp.where(col[:, :piece] < live[i] - limit, s * scale, -jnp.inf)
            old = top[i]
            peak = jnp.maximum(old, jnp.max(s, axis=1, keepdims=True))
            shrink = jnp.exp(old - peak)
            w = jnp.exp(s - peak[:, :piece])
            mixed = acc[i] * wide(shrink) + dot_nn(w.astype(jnp.bfloat16), v)
            if last:
                mass = jnp.sum(total[i] * shrink, axis=1, keepdims=True)
                mass = mass + jnp.sum(w, axis=1, keepdims=True)
                mixed = (mixed * (1.0 / mass)).astype(out_ref.dtype)
                out_ref[:, i] = mixed.reshape(steps, heads, KV_RANK)
            else:
                top[i] = peak
                total[i] = total[i] * shrink
                total[i, :, :piece] += w
                acc[i] = mixed

    own_relay.wait_recv()
    take_in(me)
    for step in range(peers - 2):
        for arrival in arrivals[step]:
            arrival.wait_recv()
        relays[step].start()
        if step:
            relays[step - 1].wait_recv()
            take_in(sources[step - 1])
    def hand_over_last():
        for arrival, relay in zip(arrivals[-1], relays[-2:]):
            arrival.wait_recv()
            relay.start()

    together = functools.reduce(jnp.logical_or, [me == row for row in TOGETHER])
    pl.when(together)(hand_over_last)
    relays[peers - 3].wait_recv()
    take_in(sources[-2])
    pl.when(jnp.logical_not(together))(hand_over_last)
    take_half(sources[-1], core, False)
    for relay in relays[-2:]:
        relay.wait_recv()
    take_half(sources[-1], mate, True)
    for copy in sends:
        copy.wait_send()
    for relay in relays + [own_relay]:
        relay.wait_send()


def direct(prompt_latent, row_cache, queries, new_latent, prompt_len, assign, row_ctx):
    peers = lax.axis_size("row")
    steps, rows, heads, width = queries.shape
    rope = width - KV_RANK
    local = prompt_latent.reshape(prompt_latent.shape[1:])
    cache_t = jnp.swapaxes(row_cache, 1, 2)
    piece = local.shape[1]
    lanes = rows * rope
    packed = rows * KV_RANK + lanes
    total_n = steps * heads
    bf16, f32 = jnp.bfloat16, jnp.float32
    hbm = pl.BlockSpec(memory_space=pl.ANY)
    smem = pl.BlockSpec(memory_space=pltpu.SMEM)
    return pl.pallas_call(
        functools.partial(fused, (NOPE_DIM + ROPE_DIM) ** (-0.5)),
        out_shape=pltpu.VMEM((steps, rows, heads, KV_RANK), bf16),
        in_specs=[hbm, hbm, hbm, hbm, smem, smem, smem],
        out_specs=pl.BlockSpec(memory_space=pltpu.VMEM),
        scratch_shapes=[
            pltpu.VMEM(local.shape, bf16),
            pltpu.VMEM(cache_t.shape, bf16),
            pltpu.VMEM(queries.shape, bf16),
            pltpu.VMEM(new_latent.shape, bf16),
            pltpu.VMEM((rows, lanes, width), bf16),
            pltpu.VMEM((rows, total_n, lanes), bf16),
            pltpu.VMEM((peers - 1, piece, packed), bf16),
            pltpu.VMEM((peers, 2, piece, packed), bf16),
            pltpu.VMEM((rows, total_n, KV_RANK), f32),
            pltpu.VMEM((rows, total_n, lanes), f32),
            pltpu.VMEM((rows, total_n, lanes), f32),
            pltpu.SemaphoreType.DMA((3,)),
            pltpu.SemaphoreType.DMA((4,)),
            pltpu.SemaphoreType.DMA((peers - 1, 2)),
            pltpu.SemaphoreType.DMA((peers, 2)),
            pltpu.SemaphoreType.DMA((peers + 1,)),
            pltpu.SemaphoreType.DMA((peers + 1,)),
            pltpu.SemaphoreType.REGULAR((peers,)),
        ],
        compiler_params=pltpu.CompilerParams(collective_id=0, has_side_effects=True),
    )(local, cache_t, queries, new_latent, prompt_len, assign, row_ctx)


def solution(mesh):
    one_group = mesh.shape["row"] == SPR and mesh.shape["tp"] == 2
    return jax.shard_map(
        direct if one_group else shards,
        mesh=mesh,
        in_specs=(
            P(("group", "row"), None, "tp", None),
            P(("group", "row"), None, None),
            P(None, ("group", "row"), "tp", None),
            P(None, ("group", "row"), None),
            P("group"),
            P("group"),
            P(("group", "row")),
        ),
        out_specs=P(None, ("group", "row"), "tp", None),
        check_vma=False,
    )
```

```python
import functools

import jax
import jax.numpy as jnp
from jax import lax
from jax.experimental import pallas as pl
from jax.experimental.pallas import tpu as pltpu
from jax.sharding import PartitionSpec as P

KV_RANK = 512
ROPE_DIM = 64
NOPE_DIM = 128
SPR = 8


def pick(array, index):
    return lax.map(lambda i: lax.dynamic_index_in_dim(array, i, 0, keepdims=False), index)


def shards(prompt_latent, row_cache, queries, new_latent, prompt_len, assign, row_ctx):
    row_count = lax.axis_size("row")
    pair_count = lax.axis_size("tp")
    row_place = lax.axis_index("row")
    rows_here = row_cache.shape[0]
    group_rows = prompt_latent.shape[1]
    piece_len = prompt_latent.shape[2]
    latent_width = prompt_latent.shape[3]
    full_len = piece_len * SPR * pair_count
    most_slots = min(rows_here, max(2, 2 * rows_here * SPR // row_count))
    home_group = row_place // SPR
    dest_prompt = assign.reshape(row_count, rows_here)
    in_group = dest_prompt // group_rows == home_group
    row_ids = jnp.arange(rows_here, dtype=jnp.int32)
    up_to = row_ids[:, None] <= row_ids[None, :]
    rank = jnp.sum((in_group[:, :, None] & up_to[None]).astype(jnp.int32), axis=1) - 1
    slot_ids = jnp.arange(most_slots, dtype=jnp.int32)
    picked = in_group[:, :, None] & (rank[:, :, None] == slot_ids[None, None, :])
    local_id = dest_prompt - home_group * group_rows
    source_index = jnp.sum(jnp.where(picked, local_id[:, :, None], 0), axis=1)
    filled = jnp.any(picked, axis=1).reshape(-1)
    owned = lax.dynamic_slice_in_dim(assign, row_place * rows_here, rows_here)
    owned_group = owned // group_rows
    same_before = (owned_group[:, None] == owned_group[None, :]) & (
        row_ids[None, :] < row_ids[:, None]
    )
    own_rank = jnp.sum(same_before.astype(jnp.int32), axis=1)
    block_ids = jnp.arange(SPR, dtype=jnp.int32)
    fetch_index = (
        (owned_group[:, None] * SPR + block_ids[None, :]) * most_slots + own_rank[:, None]
    ).reshape(-1)
    local = prompt_latent[0]
    rows_taken = pick(local, source_index.reshape(-1))
    rows_taken = jnp.where(filled[:, None, None], rows_taken, jnp.zeros_like(rows_taken))
    moved = lax.all_to_all(
        rows_taken.reshape((row_count, most_slots) + local.shape[1:]),
        "row",
        split_axis=0,
        concat_axis=0,
        tiled=True,
    )
    flat = moved.reshape(row_count * most_slots, piece_len, latent_width)
    mine = pick(flat, fetch_index).reshape(rows_here, SPR, 1, piece_len, latent_width)
    paired = lax.all_gather(mine, "tp", axis=2, tiled=True)
    latents = paired.reshape(rows_here, full_len, latent_width)
    live_len = pick(prompt_len, owned)
    scale_factor = (NOPE_DIM + ROPE_DIM) ** (-0.5)
    steps_count = queries.shape[0]
    cache_len = row_cache.shape[1]
    cache_scores = (
        jnp.einsum("srhc,rkc->rshk", queries, row_cache, preferred_element_type=jnp.float32)
        * scale_factor
    )
    cache_live = jnp.arange(cache_len, dtype=jnp.int32)[None, :] < row_ctx[:, None]
    cache_scores = jnp.where(cache_live[:, None, None, :], cache_scores, -jnp.inf)
    fresh_scores = (
        jnp.einsum("srhc,jrc->rshj", queries, new_latent, preferred_element_type=jnp.float32)
        * scale_factor
    )
    step_ids = jnp.arange(steps_count, dtype=jnp.int32)
    causal = step_ids[None, :] <= step_ids[:, None]
    fresh_scores = jnp.where(causal[None, :, None, :], fresh_scores, -jnp.inf)
    prompt_live = jnp.arange(full_len, dtype=jnp.int32)[None, :] < live_len[:, None]
    prompt_scores = (
        jnp.einsum("srhc,rkc->rshk", queries, latents, preferred_element_type=jnp.float32)
        * scale_factor
    )
    prompt_scores = jnp.where(prompt_live[:, None, None, :], prompt_scores, -jnp.inf)
    row_top = jnp.maximum(
        jnp.max(prompt_scores, axis=3, keepdims=True),
        jnp.maximum(
            jnp.max(cache_scores, axis=3, keepdims=True),
            jnp.max(fresh_scores, axis=3, keepdims=True),
        ),
    )
    prompt_exp = jnp.exp(prompt_scores - row_top)
    cache_exp = jnp.exp(cache_scores - row_top)
    fresh_exp = jnp.exp(fresh_scores - row_top)
    denominator = (
        jnp.sum(prompt_exp, axis=3, keepdims=True)
        + jnp.sum(cache_exp, axis=3, keepdims=True)
        + jnp.sum(fresh_exp, axis=3, keepdims=True)
    )
    prompt_probs = (prompt_exp / denominator).astype(jnp.bfloat16)
    cache_probs = (cache_exp / denominator).astype(jnp.bfloat16)
    fresh_probs = (fresh_exp / denominator).astype(jnp.bfloat16)
    cache_out = jnp.einsum(
        "rshk,rkc->srhc", cache_probs, row_cache[:, :, :KV_RANK], preferred_element_type=jnp.float32
    )
    fresh_out = jnp.einsum(
        "rshj,jrc->srhc",
        fresh_probs,
        new_latent[:, :, :KV_RANK],
        preferred_element_type=jnp.float32,
    )
    prompt_out = jnp.einsum(
        "rshk,rkc->srhc", prompt_probs, latents[:, :, :KV_RANK], preferred_element_type=jnp.float32
    )
    return (prompt_out + cache_out + fresh_out).astype(jnp.bfloat16)


MESH = pl.DeviceIdType.MESH


LEVELS = (1, 0, 0, 2)
SENDS = (
    (4, 5, 2, 3, 1, 6, 7),
    (5, 4, 3, 2, 0, 7, 6),
    (4, 5, 3, 0, 1, 6, 7),
    (5, 4, 2, 1, 0, 7, 6),
    (3, 0, 1, 2, 5, 6, 7),
    (2, 0, 1, 3, 4, 7, 6),
    (2, 3, 4, 5, 0, 1, 7),
    (3, 2, 5, 4, 1, 0, 6),
)
TAKES = (
    (1, 2, 3, 4, 5, 6, 7),
    (0, 3, 2, 7, 6, 5, 4),
    (3, 6, 7, 5, 0, 1, 4),
    (2, 7, 6, 4, 1, 0, 5),
    (0, 1, 5, 2, 6, 7, 3),
    (1, 0, 4, 3, 7, 6, 2),
    (7, 4, 5, 0, 1, 2, 3),
    (6, 5, 4, 1, 0, 3, 2),
)
TOGETHER = (1,)


def by_rank(rank, a, b, c, d):
    high, low = rank // 2, rank % 2
    return (1 - high) * ((1 - low) * a + low * b) + high * ((1 - low) * c + low * d)


def peers_of(me, table):
    rank, side = me // 2, me % 2
    return [(1 - side) * by_rank(rank, *step[::2]) + side * by_rank(rank, *step[1::2]) for step in zip(*table)]


def fused(
    scale,
    prompt_hbm,
    cache_hbm,
    query_hbm,
    fresh_hbm,
    plen_ref,
    assign_ref,
    ctx_ref,
    out_ref,
    prompt_v,
    cache_v,
    query_v,
    fresh_v,
    fresh_keys,
    query_rope,
    send,
    recv,
    acc,
    top,
    total,
    load_sem,
    prompt_sem,
    send_sem,
    recv_sem,
    relay_sem,
    relayed_sem,
    ready,
):
    me = lax.axis_index("row")
    core = lax.axis_index("tp")
    mate = 1 - core
    targets, sources = peers_of(me, SENDS), peers_of(me, TAKES)
    peers = len(targets) + 1
    rows = cache_v.shape[0]
    cache_len = cache_v.shape[2]
    steps, _, heads, width = query_v.shape
    rope = width - KV_RANK
    piece = prompt_v.shape[1]
    block = 2 * piece
    lanes = rows * rope
    queries_n = steps * heads

    loads = [
        pltpu.make_async_copy(source, target, load_sem.at[i])
        for i, (source, target) in enumerate(
            (
                (query_hbm, query_v),
                (cache_hbm, cache_v),
                (fresh_hbm, fresh_v),
            )
        )
    ]
    groups = prompt_v.shape[0] // 4
    prompt_loads = [
        pltpu.make_async_copy(
            prompt_hbm.at[pl.ds(i * groups, groups)],
            prompt_v.at[pl.ds(i * groups, groups)],
            prompt_sem.at[i],
        )
        for i in range(4)
    ]
    for load in prompt_loads:
        load.start()

    barrier = pltpu.get_barrier_semaphore()

    def tell(semaphore, row):
        pl.semaphore_signal(semaphore, inc=1, device_id={"row": row}, device_id_type=MESH)

    pl.semaphore_signal(barrier, inc=1, device_id={"tp": mate}, device_id_type=MESH)
    level = by_rank(me // 2, *LEVELS)
    row_levels = [LEVELS[row // 2] for row in range(peers)]
    for row, its in enumerate(row_levels):

        @pl.when((row != me) & (its >= level))
        def _():
            tell(barrier, row)

    pl.semaphore_wait(barrier, by_rank(me // 2, *(sum(its <= LEVELS[r] for its in row_levels) for r in range(4))))
    for row, its in enumerate(row_levels):

        @pl.when(its < level)
        def _():
            tell(ready.at[me], row)

    for load in prompt_loads:
        load.wait()

    def pack(dest, target):
        tails = []
        for i in range(rows):
            taken = prompt_v[assign_ref[dest * rows + i]]
            target[:, i * KV_RANK : (i + 1) * KV_RANK] = taken[:, :KV_RANK]
            tails.append(taken[:, KV_RANK:])
        target[:, rows * KV_RANK :] = jnp.concatenate(tails, axis=1)

    early = piece // 2
    cuts = [pl.ds(0, early), pl.ds(early, piece - early)]
    whole = pl.ds(0, piece)

    def copy_to(step, target, source, cut):
        return pltpu.make_async_remote_copy(
            src_ref=send.at[step, cuts[cut]],
            dst_ref=recv.at[source, core, cuts[cut]],
            send_sem=send_sem.at[step, cut],
            recv_sem=recv_sem.at[source, cut],
            device_id={"row": target},
            device_id_type=MESH,
        )

    def relay_of(step, source, part):
        return pltpu.make_async_remote_copy(
            src_ref=recv.at[source, core, part],
            dst_ref=recv.at[source, core, part],
            send_sem=relay_sem.at[step],
            recv_sem=relayed_sem.at[step],
            device_id={"tp": mate},
            device_id_type=MESH,
        )

    sends = []
    for step, target in enumerate(targets):
        pack(target, send.at[step])

        @pl.when(by_rank(target // 2, *LEVELS) > level)
        def _():
            pl.semaphore_wait(ready.at[target], 1)

        for cut in range(2):
            copy = copy_to(step, target, me, cut)
            copy.start()
            sends.append(copy)
    for load in loads:
        load.start()
    arrivals = [[copy_to(step, source, source, cut) for cut in range(2)] for step, source in enumerate(sources)]
    relays = [relay_of(step, source, whole) for step, source in enumerate(sources[:-1])]
    relays += [relay_of(peers - 2 + cut, sources[-1], cuts[cut]) for cut in range(2)]
    own_relay = relay_of(peers, me, whole)
    pack(me, recv.at[me, core])
    own_relay.start()
    fresh_keys[...] = jnp.zeros_like(fresh_keys)
    query_rope[...] = jnp.zeros_like(query_rope)

    for load in loads:
        load.wait()
    nt = (((1,), (1,)), ((), ()))

    def dot_nt(a, b):
        return lax.dot_general(a, b, nt, preferred_element_type=jnp.float32)

    def dot_nn(a, b):
        return jnp.dot(a, b, preferred_element_type=jnp.float32)

    def wide(x):
        return jnp.concatenate([x] * (KV_RANK // lanes), axis=1)

    col = lax.broadcasted_iota(jnp.int32, (queries_n, lanes), 1)
    step_of = lax.broadcasted_iota(jnp.int32, (queries_n, lanes), 0) // heads
    live = [plen_ref[assign_ref[me * rows + i]] for i in range(rows)]
    for i in range(rows):
        q = query_v[:, i].reshape(queries_n, width)
        q_nope, q_rope = q[:, :KV_RANK], q[:, KV_RANK:]
        query_rope[i, :, i * rope : (i + 1) * rope] = q_rope
        fresh_keys[i, :steps, :] = fresh_v[:, i, :]
        ctx = ctx_ref[i]
        parts = []
        values = []
        for first in range(0, cache_len, lanes):
            keys = cache_v[i, :, first : first + lanes]
            s = dot_nn(q_nope, keys[:KV_RANK]) + dot_nn(q_rope, keys[KV_RANK:])
            parts.append(jnp.where(col + first < ctx, s * scale, -jnp.inf))
            values.append(keys[:KV_RANK])
        keys = fresh_keys[i]
        s = dot_nt(q_nope, keys[:, :KV_RANK]) + dot_nt(q_rope, keys[:, KV_RANK:])
        parts.append(jnp.where(col <= step_of, s * scale, -jnp.inf))
        peak = parts[0]
        for s in parts[1:]:
            peak = jnp.maximum(peak, s)
        peak = jnp.broadcast_to(jnp.max(peak, axis=1, keepdims=True), (queries_n, lanes))
        top[i] = peak
        weights = [jnp.exp(s - peak) for s in parts]
        total[i] = sum(weights[1:], weights[0])
        out = dot_nn(weights[-1].astype(jnp.bfloat16), keys[:, :KV_RANK])
        for w, v in zip(weights, values):
            out = out + dot_nt(w.astype(jnp.bfloat16), v)
        acc[i] = out

    def take_in(source):
        limit = source * block
        for i in range(rows):
            keys = recv[source].reshape(block, rows * KV_RANK + lanes)
            q_nope = query_v[:, i].reshape(queries_n, width)[:, :KV_RANK]
            v = keys[:, i * KV_RANK : (i + 1) * KV_RANK]
            s = dot_nt(q_nope, v) + dot_nt(query_rope[i], keys[:, rows * KV_RANK :])
            s = jnp.where(col < live[i] - limit, s * scale, -jnp.inf)
            old = top[i]
            peak = jnp.maximum(old, jnp.max(s, axis=1, keepdims=True))
            shrink = jnp.exp(old - peak)
            w = jnp.exp(s - peak)
            top[i] = peak
            total[i] = total[i] * shrink + w
            acc[i] = acc[i] * wide(shrink) + dot_nn(w.astype(jnp.bfloat16), v)

    def take_half(source, half, last):
        limit = source * block + half * piece
        for i in range(rows):
            keys = recv[source, half]
            q_nope = query_v[:, i].reshape(queries_n, width)[:, :KV_RANK]
            v = keys[:, i * KV_RANK : (i + 1) * KV_RANK]
            s = dot_nt(q_nope, v) + dot_nt(query_rope[i], keys[:, rows * KV_RANK :])
            s = jnp.where(col[:, :piece] < live[i] - limit, s * scale, -jnp.inf)
            old = top[i]
            peak = jnp.maximum(old, jnp.max(s, axis=1, keepdims=True))
            shrink = jnp.exp(old - peak)
            w = jnp.exp(s - peak[:, :piece])
            mixed = acc[i] * wide(shrink) + dot_nn(w.astype(jnp.bfloat16), v)
            if last:
                mass = jnp.sum(total[i] * shrink, axis=1, keepdims=True)
                mass = mass + jnp.sum(w, axis=1, keepdims=True)
                mixed = (mixed * (1.0 / mass)).astype(out_ref.dtype)
                out_ref[:, i] = mixed.reshape(steps, heads, KV_RANK)
            else:
                top[i] = peak
                total[i] = total[i] * shrink
                total[i, :, :piece] += w
                acc[i] = mixed

    own_relay.wait_recv()
    take_in(me)
    for step in range(peers - 2):
        for arrival in arrivals[step]:
            arrival.wait_recv()
        relays[step].start()
        if step:
            relays[step - 1].wait_recv()
            take_in(sources[step - 1])
    def hand_over_last():
        for arrival, relay in zip(arrivals[-1], relays[-2:]):
            arrival.wait_recv()
            relay.start()

    together = functools.reduce(jnp.logical_or, [me == row for row in TOGETHER])
    pl.when(together)(hand_over_last)
    relays[peers - 3].wait_recv()
    take_in(sources[-2])
    pl.when(jnp.logical_not(together))(hand_over_last)
    take_half(sources[-1], core, False)
    for relay in relays[-2:]:
        relay.wait_recv()
    take_half(sources[-1], mate, True)
    for copy in sends:
        copy.wait_send()
    for relay in relays + [own_relay]:
        relay.wait_send()


def direct(prompt_latent, row_cache, queries, new_latent, prompt_len, assign, row_ctx):
    peers = lax.axis_size("row")
    steps, rows, heads, width = queries.shape
    rope = width - KV_RANK
    local = prompt_latent.reshape(prompt_latent.shape[1:])
    cache_t = jnp.swapaxes(row_cache, 1, 2)
    piece = local.shape[1]
    lanes = rows * rope
    packed = rows * KV_RANK + lanes
    total_n = steps * heads
    bf16, f32 = jnp.bfloat16, jnp.float32
    hbm = pl.BlockSpec(memory_space=pl.ANY)
    smem = pl.BlockSpec(memory_space=pltpu.SMEM)
    return pl.pallas_call(
        functools.partial(fused, (NOPE_DIM + ROPE_DIM) ** (-0.5)),
        out_shape=pltpu.VMEM((steps, rows, heads, KV_RANK), bf16),
        in_specs=[hbm, hbm, hbm, hbm, smem, smem, smem],
        out_specs=pl.BlockSpec(memory_space=pltpu.VMEM),
        scratch_shapes=[
            pltpu.VMEM(local.shape, bf16),
            pltpu.VMEM(cache_t.shape, bf16),
            pltpu.VMEM(queries.shape, bf16),
            pltpu.VMEM(new_latent.shape, bf16),
            pltpu.VMEM((rows, lanes, width), bf16),
            pltpu.VMEM((rows, total_n, lanes), bf16),
            pltpu.VMEM((peers - 1, piece, packed), bf16),
            pltpu.VMEM((peers, 2, piece, packed), bf16),
            pltpu.VMEM((rows, total_n, KV_RANK), f32),
            pltpu.VMEM((rows, total_n, lanes), f32),
            pltpu.VMEM((rows, total_n, lanes), f32),
            pltpu.SemaphoreType.DMA((3,)),
            pltpu.SemaphoreType.DMA((4,)),
            pltpu.SemaphoreType.DMA((peers - 1, 2)),
            pltpu.SemaphoreType.DMA((peers, 2)),
            pltpu.SemaphoreType.DMA((peers + 1,)),
            pltpu.SemaphoreType.DMA((peers + 1,)),
            pltpu.SemaphoreType.REGULAR((peers,)),
        ],
        compiler_params=pltpu.CompilerParams(collective_id=0, has_side_effects=True),
    )(local, cache_t, queries, new_latent, prompt_len, assign, row_ctx)


def solution(mesh):
    one_group = mesh.shape["row"] == SPR and mesh.shape["tp"] == 2
    return jax.shard_map(
        direct if one_group else shards,
        mesh=mesh,
        in_specs=(
            P(("group", "row"), None, "tp", None),
            P(("group", "row"), None, None),
            P(None, ("group", "row"), "tp", None),
            P(None, ("group", "row"), None),
            P("group"),
            P("group"),
            P(("group", "row")),
        ),
        out_specs=P(None, ("group", "row"), "tp", None),
        check_vma=False,
    )
```
